256 devices in a mesh: row: 16 (over x, z_lo), col: 16 (over z_hi, y, core).
Axes of the slice: x: 4, y: 4, z: 8 (z_hi: 2, z_lo: 4; z = z_hi * 4 + z_lo), core: 2. Of those that a mesh axis runs over, the one named last changes fastest.
Arguments:
- tensor: float32 [32, 2048, 4096], P(None, 'row', 'col'), may hold values from -6 to 6
- initial_first: float32 [2048, 256], P('row'), may hold values from -6 to 6
- initial_second: float32 [4096, 256], P('col'), may hold values from -6 to 6
Outputs:
- factor_first: float32 [2048, 256], P('row')
- factor_second: float32 [4096, 256], P('col')
- factor_frames: float32 [32, 256], replicated
- weights: float32 [256], replicated
The draws below stay inside these ranges and needn't reach their ends.
All inputs are finite; a program needn't handle non-finite values.
Results may differ from the reference program's by a relative error of at most 0.00024.
Values sent between devices are 32-bit elements; how exact they have to be, the bound alone decides.
No kernel may reach another device: no remote copies, remote signals or barrier semaphores. Data moves between devices by JAX's collectives and lax.ppermute only.
A program may use at most 128 MiB of HBM per device.

```python
import math
import jax
import jax.numpy as jnp
from jax import lax

R = 256
K = 32
PASSES = 2
I = 2048
J = 4096


def block_scale(stream_key, shape, shards, least, high):
    factor_of = 1.0
    for position, parts in shards:
        draws = jax.random.uniform(jax.random.fold_in(jax.random.fold_in(stream_key, 6), position), (parts,), jnp.float32, least / len(shards), high / len(shards))
        factor_of = factor_of * jnp.repeat(jnp.exp(draws), shape[position] // parts).reshape((-1,) + (1,) * (len(shape) - 1 - position))
    return factor_of


def scatter_about(own_key, shape, scale, reach, split=(), dtype=jnp.bfloat16):
    array = jax.random.normal(own_key, shape, jnp.float32) * scale
    if len(split) > 0:
        array = block_scale(own_key, shape, split, -0.22, 0.18) * array
    return jnp.clip(array, min=-reach, max=reach).astype(dtype)


def setup_inputs(seed: int = 0) -> dict:
    seeds = jax.random.split(jax.random.key(seed), 4)
    return {
        "tensor": scatter_about(seeds[0], (K, I, J), 1.0, 6.0, ((1, 16), (2, 16)), jnp.float32),
        "initial_first": scatter_about(seeds[1], (I, R), 1.0, 6.0, ((0, 16),), jnp.float32),
        "initial_second": scatter_about(seeds[2], (J, R), 1.0, 6.0, ((0, 16),), jnp.float32),
    }


epsilon = 1e-06

def solve_gram(partials, hadamard):
    factor_lower = jnp.linalg.cholesky(hadamard)
    midway = lax.linalg.triangular_solve(factor_lower, partials, left_side=False, lower=True, transpose_a=True)
    return lax.linalg.triangular_solve(factor_lower, midway, left_side=False, lower=True, transpose_a=False)

def normalize(unscaled):
    scaling = jnp.sqrt(lax.optimization_barrier(jnp.mean(unscaled * unscaled, axis=0)) + epsilon)
    return (unscaled / scaling, scaling)

def gram_of(matrix):
    return jnp.dot(matrix.T, matrix, precision=lax.Precision.HIGHEST) / matrix.shape[0]

def reference(tensor, initial_first, initial_second):
    highest = lax.Precision.HIGHEST
    frames = tensor.shape[0]
    rows_first = tensor.shape[1]
    rows_second = tensor.shape[2]
    first_gram = gram_of(initial_first)
    second = initial_second
    second_gram = gram_of(initial_second)
    contracted = jnp.einsum('kij,ir->kjr', tensor, initial_first, precision=highest)
    for repeat in range(PASSES):
        frame_sums = jnp.einsum('kjr,jr->kr', contracted, second, precision=highest)
        frame_raw = solve_gram(frame_sums, first_gram * second_gram) / math.sqrt(rows_first * rows_second)
        factor_frames, unused = normalize(frame_raw)
        frame_gram = gram_of(factor_frames)
        second_sums = jnp.einsum('kjr,kr->jr', contracted, factor_frames, precision=highest)
        second_raw = solve_gram(second_sums, first_gram * frame_gram) / math.sqrt(rows_first * frames)
        second, unused = normalize(second_raw)
        second_gram = gram_of(second)
    second_contracted = jnp.einsum('kij,jr->kir', tensor, second, precision=highest)
    first_sums = jnp.einsum('kir,kr->ir', second_contracted, factor_frames, precision=highest)
    first_raw = solve_gram(first_sums, second_gram * frame_gram) / math.sqrt(rows_second * frames)
    factor_first, weights = normalize(first_raw)
    return (factor_first, second, factor_frames, weights)
```

```python
import functools
import math

import jax
import jax.numpy as jnp
from jax import lax
from jax.experimental import pallas as pl
from jax.experimental.pallas import tpu as pltpu
from jax.sharding import PartitionSpec as P

PASSES = 2
BLOCK = 64

epsilon = 1e-06
HIGHEST = lax.Precision.HIGHEST
HIGH = lax.Precision.HIGH


def dot(a, b):
    return jnp.dot(a, b, precision=HIGHEST, preferred_element_type=jnp.float32)


def invert_small(x, n):
    sub = lax.broadcasted_iota(jnp.int32, (n, n), 0)
    lane = lax.broadcasted_iota(jnp.int32, (n, n), 1)
    lane_row = lax.broadcasted_iota(jnp.int32, (1, n), 1)
    for p in range(0, n, 2):
        c0 = jnp.broadcast_to(x[:, p : p + 1], (n, n))
        c1 = jnp.broadcast_to(x[:, p + 1 : p + 2], (n, n))
        a, b, d = c0[p : p + 1, :], c0[p + 1 : p + 2, :], c1[p + 1 : p + 2, :]
        e0, e1 = lane_row == p, lane_row == p + 1
        r0 = jnp.where(e0, 1.0, jnp.where(e1, 0.0, x[p : p + 1, :]))
        r1 = jnp.where(e1, 1.0, jnp.where(e0, 0.0, x[p + 1 : p + 2, :]))
        over = 1.0 / (a * d - b * b)
        q0 = (d * r0 - b * r1) * over
        q1 = (a * r1 - b * r0) * over
        rest = jnp.where((lane == p) | (lane == p + 1), 0.0, x) - c0 * q0 - c1 * q1
        x = jnp.where(sub == p, q0, jnp.where(sub == p + 1, q1, rest))
    return x


def invert_kernel(v_ref, w_ref):
    n = v_ref.shape[0]
    v = v_ref[...]
    lane_n = lax.broadcasted_iota(jnp.int32, (n, n), 1)
    diagonal = jnp.where(lane_n == lax.broadcasted_iota(jnp.int32, (n, n), 0), v, 0.0)
    over_row = lax.rsqrt(jnp.sum(diagonal, axis=0, keepdims=True))
    over_col = lax.rsqrt(jnp.sum(diagonal, axis=1, keepdims=True))
    v = v * over_row * over_col
    lane = lax.broadcasted_iota(jnp.int32, (BLOCK, n), 1)
    sub = lax.broadcasted_iota(jnp.int32, (BLOCK, n), 0)
    for p in range(0, n, BLOCK):
        pivot = invert_small(v[p : p + BLOCK, p : p + BLOCK], BLOCK)
        inside = (lane >= p) & (lane < p + BLOCK)
        rows = jnp.where(inside, jnp.where(lane - p == sub, 1.0, 0.0), v[p : p + BLOCK, :])
        q = dot(pivot, rows)
        cleared = jnp.where((lane_n >= p) & (lane_n < p + BLOCK), 0.0, v)
        rest = cleared - dot(v[:, p : p + BLOCK], q)
        parts = [rest[:p], q, rest[p + BLOCK :]]
        v = jnp.concatenate([part for part in parts if part.shape[0] > 0], 0)
    w_ref[...] = v * over_row * over_col


def invert(v):
    n = v.shape[0]
    vmem = pl.BlockSpec(memory_space=pltpu.VMEM)
    return pl.pallas_call(
        invert_kernel,
        out_shape=jax.ShapeDtypeStruct(v.shape, jnp.float32),
        in_specs=[vmem],
        out_specs=vmem,
        compiler_params=pltpu.CompilerParams(vmem_limit_bytes=16 << 20),
        name="invert",
    )(v)


def all_sum(x, axis):
    size = lax.axis_size(axis)
    step = 1
    while step < size:
        x = x + lax.ppermute(x, axis, [(i, i ^ step) for i in range(size)])
        step *= 2
    return x


def gram(matrix):
    return lax.dot_general(
        matrix, matrix, (((0,), (0,)), ((), ())), precision=HIGHEST, preferred_element_type=jnp.float32
    )


def body(tensor, initial_first, initial_second):
    frames = tensor.shape[0]
    rows_first = tensor.shape[1] * lax.axis_size("row")
    rows_second = tensor.shape[2] * lax.axis_size("col")
    first_gram = all_sum(gram(initial_first), "row") / rows_first
    second_gram = all_sum(gram(initial_second), "col") / rows_second
    contracted = jnp.einsum("kij,ir->kjr", tensor, initial_first, precision=HIGH)
    unscaled = initial_second
    scaling = None
    for repeat in range(PASSES):
        frame_terms = jnp.sum(contracted * unscaled[None], axis=1)
        frame_sums = all_sum(all_sum(frame_terms, "row"), "col")
        if scaling is not None:
            frame_sums = frame_sums / scaling
        frame_raw = dot(frame_sums, invert(first_gram * second_gram)) / math.sqrt(
            rows_first * rows_second
        )
        frame_scaling = jnp.sqrt(jnp.mean(frame_raw * frame_raw, axis=0) + epsilon)
        factor_frames = frame_raw / frame_scaling
        frame_gram = gram(factor_frames) / frames
        second_terms = jnp.sum(contracted * factor_frames[:, None, :], axis=0)
        inverse = invert(first_gram * frame_gram)
        second_sums = all_sum(second_terms, "row")
        unscaled = dot(second_sums, inverse) / math.sqrt(rows_first * frames)
        raw_gram = all_sum(gram(unscaled), "col") / rows_second
        diagonal = jnp.sum(jnp.where(jnp.eye(raw_gram.shape[0], dtype=bool), raw_gram, 0.0), axis=0)
        scaling = jnp.sqrt(diagonal + epsilon)
        second_gram = raw_gram / (scaling[:, None] * scaling[None, :])
    second_contracted = jnp.einsum("kij,jr->kir", tensor, unscaled, precision=HIGH)
    first_terms = jnp.sum(second_contracted * factor_frames[:, None, :], axis=0)
    first_sums = all_sum(first_terms, "col") / scaling
    inverse = invert(second_gram * frame_gram)
    first_raw = dot(first_sums, inverse) / math.sqrt(rows_second * frames)
    squares = all_sum(jnp.sum(first_raw * first_raw, axis=0, keepdims=True), "row")[0]
    weights = jnp.sqrt(squares / rows_first + epsilon)
    return (first_raw / weights, unscaled / scaling, factor_frames, weights)


def solution(mesh):
    placed = (P(None, "row", "col"), P("row", None), P("col", None))
    return jax.shard_map(
        body,
        mesh=mesh,
        in_specs=placed,
        out_specs=(P("row", None), P("col", None), P(), P()),
        check_vma=False,
    )
```

```python
import functools
import math

import jax
import jax.numpy as jnp
from jax import lax
from jax.experimental import pallas as pl
from jax.experimental.pallas import tpu as pltpu
from jax.sharding import PartitionSpec as P

PASSES = 2
BLOCK = 64
QUARTER = 4

ROW_X = (4, 8, 12)
ROW_Z = (1, 2, 3)
COL_CORE = (1,)
COL_Y = (2, 4, 6)
COL_Z = (8,)

epsilon = 1e-06
HIGHEST = lax.Precision.HIGHEST
HIGH = lax.Precision.HIGH
VMEM = pl.BlockSpec(memory_space=pltpu.VMEM)
SMEM = pl.BlockSpec(memory_space=pltpu.SMEM)
F32 = jnp.float32


def dot(a, b, dims=((1,), (0,))):
    return lax.dot_general(a, b, (dims, ((), ())), precision=HIGHEST, preferred_element_type=F32)


def gram(matrix):
    return dot(matrix, matrix, ((0,), (0,)))


def call(kernel, name, outs, in_specs, flops=0, limit=16):
    return pl.pallas_call(
        kernel,
        out_shape=tuple(jax.ShapeDtypeStruct(shape, F32) for shape in outs),
        in_specs=in_specs,
        out_specs=tuple(VMEM for shape in outs),
        compiler_params=pltpu.CompilerParams(vmem_limit_bytes=limit << 20),
        cost_estimate=pl.CostEstimate(flops=flops, bytes_accessed=1 << 18, transcendentals=0),
        name=name,
    )


def partners(x, axis, masks):
    size = lax.axis_size(axis)
    return [lax.ppermute(x, axis, [(i, i ^ mask) for i in range(size)]) for mask in masks]


def tree(terms):
    while len(terms) > 1:
        terms = [terms[i] + terms[i + 1] for i in range(0, len(terms), 2)]
    return terms[0]


def sum_over(x, axis, masks):
    return tree([x] + partners(x, axis, masks))


def tie(*values):
    return lax.optimization_barrier(values)


def invert_pair(a, b, d):
    over = 1.0 / (a * d - b * b)
    return d * over, -b * over, a * over


def invert_small(x, n):
    sub = lax.broadcasted_iota(jnp.int32, (n, n), 0)
    lane = lax.broadcasted_iota(jnp.int32, (n, n), 1)
    lane_row = lax.broadcasted_iota(jnp.int32, (1, n), 1)
    for p in range(0, n, 4):
        c = [jnp.broadcast_to(x[:, p + j : p + j + 1], (n, n)) for j in range(4)]
        a = [[c[j][p + i : p + i + 1, :] for j in range(4)] for i in range(4)]
        inside = (lane_row >= p) & (lane_row < p + 4)
        r = [
            jnp.where(inside, jnp.where(lane_row == p + i, 1.0, 0.0), x[p + i : p + i + 1, :])
            for i in range(4)
        ]
        i00, i01, i11 = invert_pair(a[0][0], a[1][0], a[1][1])
        t20 = a[2][0] * i00 + a[2][1] * i01
        t21 = a[2][0] * i01 + a[2][1] * i11
        t30 = a[3][0] * i00 + a[3][1] * i01
        t31 = a[3][0] * i01 + a[3][1] * i11
        s22 = a[2][2] - (t20 * a[2][0] + t21 * a[2][1])
        s23 = a[3][2] - (t30 * a[2][0] + t31 * a[2][1])
        s33 = a[3][3] - (t30 * a[3][0] + t31 * a[3][1])
        w2 = r[2] - (t20 * r[0] + t21 * r[1])
        w3 = r[3] - (t30 * r[0] + t31 * r[1])
        g0 = i00 * r[0] + i01 * r[1]
        g1 = i01 * r[0] + i11 * r[1]
        j22, j23, j33 = invert_pair(s22, s23, s33)
        q2 = j22 * w2 + j23 * w3
        q3 = j23 * w2 + j33 * w3
        q = [g0 - (t20 * q2 + t30 * q3), g1 - (t21 * q2 + t31 * q3), q2, q3]
        x = jnp.where((lane >= p) & (lane < p + 4), 0.0, x)
        x = x - ((c[0] * q[0] + c[1] * q[1]) + (c[2] * q[2] + c[3] * q[3]))
        for i in range(4):
            x = jnp.where(sub == p + i, q[i], x)
    return x


def eliminate(v, starts):
    n = v.shape[0]
    lane_n = lax.broadcasted_iota(jnp.int32, (n, n), 1)
    lane = lax.broadcasted_iota(jnp.int32, (BLOCK, n), 1)
    sub = lax.broadcasted_iota(jnp.int32, (BLOCK, n), 0)
    for p in starts:
        pivot = invert_small(v[p : p + BLOCK, p : p + BLOCK], BLOCK)
        inside = (lane >= p) & (lane < p + BLOCK)
        rows = jnp.where(inside, jnp.where(lane - p == sub, 1.0, 0.0), v[p : p + BLOCK, :])
        q = dot(pivot, rows)
        cleared = jnp.where((lane_n >= p) & (lane_n < p + BLOCK), 0.0, v)
        rest = cleared - dot(v[:, p : p + BLOCK], q)
        parts = [rest[:p], q, rest[p + BLOCK :]]
        v = jnp.concatenate([part for part in parts if part.shape[0] > 0], 0)
    return v


def diagonal_of(v):
    n = v.shape[0]
    same = lax.broadcasted_iota(jnp.int32, (n, n), 0) == lax.broadcasted_iota(jnp.int32, (n, n), 1)
    kept = jnp.where(same, v, 0.0)
    return jnp.sum(kept, axis=0, keepdims=True), jnp.sum(kept, axis=1, keepdims=True)


def begin_inverse(v, state, over_row, over_col):
    n = v.shape[0]
    along_lanes, along_rows = diagonal_of(v)
    over_lanes, over_rows = lax.rsqrt(along_lanes), lax.rsqrt(along_rows)
    over_row[...] = over_lanes
    over_col[...] = over_rows
    state[...] = eliminate(v * over_lanes * over_rows, range(0, n // 2, BLOCK))


def finish_kernel(state, over_row, over_col, inverse):
    n = state.shape[0]
    v = eliminate(state[...], range(n // 2, n, BLOCK))
    inverse[...] = v * over_row[...] * over_col[...]


def finish_inverse(state, over_row, over_col):
    n = state.shape[0]
    (inverse,) = call(finish_kernel, "finish_inverse", [(n, n)], [VMEM] * 3, flops=6 * 10**9)(
        state, over_row, over_col
    )
    return inverse


def gather_rows(position, pieces, into, rows):
    for mask, piece in enumerate(pieces):
        start = pl.multiple_of((position ^ mask) * rows, rows)
        into[pl.ds(start, rows), :] = piece[:rows, :]


def begin_first_kernel(scale_first, scale_second, where, *refs):
    firsts, seconds, (first_gram, state, over_row, over_col) = refs[:4], refs[4:8], refs[8:]
    rows = first_gram.shape[0] // QUARTER
    gather_rows(where[0], seconds, state, rows)
    gather_rows(where[1], firsts, first_gram, rows)
    grams = first_gram[...] * scale_first
    first_gram[...] = grams
    begin_inverse(grams * (state[...] * scale_second), state, over_row, over_col)


def begin_kernel(v, state, over_row, over_col):
    begin_inverse(v[...], state, over_row, over_col)


def begin_second_kernel(scale_second, where, other, *refs):
    pieces, (state, over_row, over_col, scaling) = refs[:4], refs[4:]
    n = state.shape[0]
    gather_rows(where[0], pieces, state, n // QUARTER)
    raw = state[...] * scale_second
    along_lanes, along_rows = diagonal_of(raw)
    norm_lanes = jnp.sqrt(along_lanes + epsilon)
    norm_rows = jnp.sqrt(along_rows + epsilon)
    scaling[...] = norm_lanes
    begin_inverse(other[...] * (raw / norm_lanes / norm_rows), state, over_row, over_col)


def frames_kernel(scale, scaling, inverse, first_gram, *refs):
    terms, (factor, frame_gram, hadamard) = refs[:-3], refs[-3:]
    frames = factor.shape[0]
    sums = tree([term[...] for term in terms]) / scaling[...]
    raw = dot(sums, inverse[...]) * scale
    norm = jnp.sqrt(jnp.sum(raw * raw, axis=0, keepdims=True) / frames + epsilon)
    normed = raw / norm
    factor[...] = normed
    grams = dot(normed.T, normed) / frames
    frame_gram[...] = grams
    hadamard[...] = first_gram[...] * grams


def second_kernel(with_frames, where, *refs):
    pieces, rest = refs[:4], refs[4:]
    if with_frames:
        contracted, second, payload, whole = rest
    else:
        second, payload, whole = rest
    n = second.shape[1]
    gather_rows(where[0], pieces, second, second.shape[0] // QUARTER)
    x = second[...]
    whole[...] = dot(x.T, x)
    rows = n // QUARTER
    payload[:rows, :] = whole[pl.ds(pl.multiple_of(where[0] * rows, rows), rows), :]
    if with_frames:
        for k in range(contracted.shape[0]):
            terms = jnp.sum(contracted[k] * second[...], axis=0, keepdims=True)
            payload[rows + k : rows + k + 1, :] = terms


def body(tensor, initial_first, initial_second):
    frames, block_first, block_second = tensor.shape
    rank = initial_first.shape[1]
    square, line, column = (rank, rank), (1, rank), (rank, 1)
    quarter = rank // QUARTER
    part = block_second // QUARTER
    rows_first = block_first * lax.axis_size("row")
    rows_second = block_second * lax.axis_size("col")
    at_x = lax.axis_index("row") // 4
    at_y = lax.axis_index("col") // 2 % 4
    where = jnp.stack([at_x, at_y]).astype(jnp.int32)

    firsts = lax.dynamic_slice_in_dim(gram(initial_first), at_y * quarter, quarter)
    seconds = lax.dynamic_slice_in_dim(gram(initial_second), at_x * quarter, quarter)
    firsts = sum_over(firsts, "row", ROW_X)
    seconds = sum_over(sum_over(seconds, "col", COL_CORE), "col", COL_Y)
    contracted = jnp.einsum("kij,ir->kjr", tensor, initial_first, precision=HIGH)
    terms = jnp.sum(contracted * initial_second[None], axis=1)
    both = sum_over(jnp.concatenate([firsts, terms], 0), "row", ROW_Z)
    seconds = sum_over(seconds, "col", COL_Z)
    firsts, terms = both[:quarter], both[quarter:]
    firsts = [firsts] + partners(firsts, "col", COL_Y)
    both = jnp.concatenate([seconds, terms], 0)
    both = [both] + partners(both, "row", ROW_X)
    *both, terms = tie(*both, tree([piece[quarter:] for piece in both]))
    first_gram, state, over_row, over_col = call(
        functools.partial(begin_first_kernel, 1.0 / rows_first, 1.0 / rows_second),
        "begin_first",
        [square, square, line, column],
        [SMEM] + [VMEM] * 8,
        flops=6 * 10**9,
    )(where, *firsts, *both)
    terms = sum_over(terms, "col", COL_Y)
    state, terms = tie(state, terms)
    terms = sum_over(terms, "col", COL_CORE)
    terms = [terms] + partners(terms, "col", COL_Z)
    inverse = finish_inverse(state, over_row, over_col)
    scaling = jnp.ones(line, F32)

    for repeat in range(PASSES):
        factor_frames, frame_gram, hadamard = call(
            functools.partial(frames_kernel, 1.0 / math.sqrt(rows_first * rows_second)),
            "frames",
            [(frames, rank), square, square],
            [VMEM] * (3 + len(terms)),
        )(scaling, inverse, first_gram, *terms)

        sums = jnp.sum(contracted * factor_frames[:, None, :], axis=0)
        own, *sent = [
            lax.dynamic_slice_in_dim(sums, (at_x ^ mask) * part, part) for mask in range(QUARTER)
        ]
        own, *sent, hadamard = tie(own, *sent, hadamard)
        sent = [
            lax.ppermute(piece, "row", [(i, i ^ mask) for i in range(lax.axis_size("row"))])
            for piece, mask in zip(sent, ROW_X)
        ]
        state, over_row, over_col = call(
            begin_kernel, "begin", [square, line, column], [VMEM], flops=6 * 10**9
        )(hadamard)
        own, state = tie(tree([own] + sent), state)
        sums = [own] + partners(own, "row", ROW_Z)
        inverse = finish_inverse(state, over_row, over_col)
        *sums, inverse = tie(*sums, inverse)
        piece = dot(tree(sums), inverse) * (1.0 / math.sqrt(rows_first * frames))
        pieces = [piece] + partners(piece, "row", ROW_X)

        last = repeat == PASSES - 1
        height = quarter + (0 if last else frames)
        second, payload, unused = call(
            functools.partial(second_kernel, not last),
            "second",
            [(block_second, rank), (height, rank), square],
            [SMEM] + [VMEM] * (4 if last else 5),
            limit=32,
        )(where, *pieces, *([] if last else [contracted]))
        for masks in (COL_CORE, COL_Y, COL_Z):
            payload = sum_over(payload, "col", masks)
        pieces = [payload] + partners(payload, "row", ROW_X)
        other = frame_gram if last else first_gram
        if not last:
            *pieces, terms = tie(*pieces, tree([piece[quarter:] for piece in pieces]))
            terms = [terms] + partners(terms, "row", ROW_Z)
        state, over_row, over_col, scaling = call(
            functools.partial(begin_second_kernel, 1.0 / rows_second),
            "begin_second",
            [square, line, column, line],
            [SMEM] + [VMEM] * 5,
            flops=6 * 10**9,
        )(where, other, *pieces)
        inverse = finish_inverse(state, over_row, over_col)

    contracted = jnp.einsum("kij,jr->kir", tensor, second, precision=HIGH)
    terms = jnp.sum(contracted * factor_frames[:, None, :], axis=0)
    for masks in (COL_CORE, COL_Y, COL_Z):
        terms = sum_over(terms, "col", masks)
    first_raw = dot(terms / scaling, inverse) * (1.0 / math.sqrt(rows_second * frames))
    squares = jnp.sum(first_raw * first_raw, axis=0, keepdims=True)
    squares = sum_over(sum_over(squares, "row", ROW_X), "row", ROW_Z)
    weights = jnp.sqrt(squares[0] / rows_first + epsilon)
    return (first_raw / weights, second / scaling, factor_frames, weights)


def solution(mesh):
    placed = (P(None, "row", "col"), P("row", None), P("col", None))
    return jax.shard_map(
        body,
        mesh=mesh,
        in_specs=placed,
        out_specs=(P("row", None), P("col", None), P(), P()),
        check_vma=False,
    )
```

```python
import functools
import math

import jax
import jax.numpy as jnp
from jax import lax
from jax.experimental import pallas as pl
from jax.experimental.pallas import tpu as pltpu
from jax.sharding import PartitionSpec as P

PASSES = 2
BLOCK = 64
QUARTER = 4

ROW_X = (4, 8, 12)
ROW_Z = (1, 2, 3)
COL_CORE = (1,)
COL_Y = (2, 4, 6)
COL_Z = (8,)

epsilon = 1e-06
HIGHEST = lax.Precision.HIGHEST
HIGH = lax.Precision.HIGH
VMEM = pl.BlockSpec(memory_space=pltpu.VMEM)
SMEM = pl.BlockSpec(memory_space=pltpu.SMEM)
F32 = jnp.float32


def dot(a, b, dims=((1,), (0,))):
    return lax.dot_general(a, b, (dims, ((), ())), precision=HIGHEST, preferred_element_type=F32)


def gram(matrix):
    return dot(matrix, matrix, ((0,), (0,)))


def call(kernel, name, outs, in_specs, flops=0, limit=4):
    return pl.pallas_call(
        kernel,
        out_shape=tuple(jax.ShapeDtypeStruct(shape, F32) for shape in outs),
        in_specs=in_specs,
        out_specs=tuple(VMEM for shape in outs),
        compiler_params=pltpu.CompilerParams(vmem_limit_bytes=limit << 20),
        cost_estimate=pl.CostEstimate(flops=flops, bytes_accessed=1 << 18, transcendentals=0),
        name=name,
    )


def partners(x, axis, masks):
    size = lax.axis_size(axis)
    return [lax.ppermute(x, axis, [(i, i ^ mask) for i in range(size)]) for mask in masks]


def tree(terms):
    while len(terms) > 1:
        terms = [terms[i] + terms[i + 1] for i in range(0, len(terms), 2)]
    return terms[0]


def sum_over(x, axis, masks):
    return tree([x] + partners(x, axis, masks))


def tie(*values):
    return lax.optimization_barrier(values)


def invert_pair(a, b, d):
    over = 1.0 / (a * d - b * b)
    return d * over, -b * over, a * over


def invert_small(x, n):
    sub = lax.broadcasted_iota(jnp.int32, (n, n), 0)
    lane = lax.broadcasted_iota(jnp.int32, (n, n), 1)
    lane_row = lax.broadcasted_iota(jnp.int32, (1, n), 1)
    for p in range(0, n, 4):
        c = [jnp.broadcast_to(x[:, p + j : p + j + 1], (n, n)) for j in range(4)]
        a = [[c[j][p + i : p + i + 1, :] for j in range(4)] for i in range(4)]
        inside = (lane_row >= p) & (lane_row < p + 4)
        r = [
            jnp.where(inside, jnp.where(lane_row == p + i, 1.0, 0.0), x[p + i : p + i + 1, :])
            for i in range(4)
        ]
        i00, i01, i11 = invert_pair(a[0][0], a[1][0], a[1][1])
        t20 = a[2][0] * i00 + a[2][1] * i01
        t21 = a[2][0] * i01 + a[2][1] * i11
        t30 = a[3][0] * i00 + a[3][1] * i01
        t31 = a[3][0] * i01 + a[3][1] * i11
        s22 = a[2][2] - (t20 * a[2][0] + t21 * a[2][1])
        s23 = a[3][2] - (t30 * a[2][0] + t31 * a[2][1])
        s33 = a[3][3] - (t30 * a[3][0] + t31 * a[3][1])
        w2 = r[2] - (t20 * r[0] + t21 * r[1])
        w3 = r[3] - (t30 * r[0] + t31 * r[1])
        g0 = i00 * r[0] + i01 * r[1]
        g1 = i01 * r[0] + i11 * r[1]
        j22, j23, j33 = invert_pair(s22, s23, s33)
        q2 = j22 * w2 + j23 * w3
        q3 = j23 * w2 + j33 * w3
        q = [g0 - (t20 * q2 + t30 * q3), g1 - (t21 * q2 + t31 * q3), q2, q3]
        x = jnp.where((lane >= p) & (lane < p + 4), 0.0, x)
        x = x - ((c[0] * q[0] + c[1] * q[1]) + (c[2] * q[2] + c[3] * q[3]))
        for i in range(4):
            x = jnp.where(sub == p + i, q[i], x)
    return x


def eliminate(v, starts):
    n = v.shape[0]
    lane_n = lax.broadcasted_iota(jnp.int32, (n, n), 1)
    lane = lax.broadcasted_iota(jnp.int32, (BLOCK, n), 1)
    sub = lax.broadcasted_iota(jnp.int32, (BLOCK, n), 0)
    for p in starts:
        pivot = invert_small(v[p : p + BLOCK, p : p + BLOCK], BLOCK)
        inside = (lane >= p) & (lane < p + BLOCK)
        rows = jnp.where(inside, jnp.where(lane - p == sub, 1.0, 0.0), v[p : p + BLOCK, :])
        q = dot(pivot, rows)
        cleared = jnp.where((lane_n >= p) & (lane_n < p + BLOCK), 0.0, v)
        rest = cleared - dot(v[:, p : p + BLOCK], q)
        parts = [rest[:p], q, rest[p + BLOCK :]]
        v = jnp.concatenate([part for part in parts if part.shape[0] > 0], 0)
    return v


def diagonal_of(v):
    n = v.shape[0]
    same = lax.broadcasted_iota(jnp.int32, (n, n), 0) == lax.broadcasted_iota(jnp.int32, (n, n), 1)
    kept = jnp.where(same, v, 0.0)
    return jnp.sum(kept, axis=0, keepdims=True), jnp.sum(kept, axis=1, keepdims=True)


def begin_inverse(v, state, over_row, over_col):
    n = v.shape[0]
    along_lanes, along_rows = diagonal_of(v)
    over_lanes, over_rows = lax.rsqrt(along_lanes), lax.rsqrt(along_rows)
    over_row[...] = over_lanes
    over_col[...] = over_rows
    state[...] = eliminate(v * over_lanes * over_rows, range(0, n // 2, BLOCK))


def finish_kernel(state, over_row, over_col, inverse):
    n = state.shape[0]
    v = eliminate(state[...], range(n // 2, n, BLOCK))
    inverse[...] = v * over_row[...] * over_col[...]


def finish_inverse(state, over_row, over_col):
    n = state.shape[0]
    (inverse,) = call(finish_kernel, "finish_inverse", [(n, n)], [VMEM] * 3, flops=10**6)(
        state, over_row, over_col
    )
    return inverse


def gather_rows(position, pieces, into, rows):
    for mask, piece in enumerate(pieces):
        start = pl.multiple_of((position ^ mask) * rows, rows)
        into[pl.ds(start, rows), :] = piece[:rows, :]


def pack_symmetric(g, packed):
    n = g.shape[0]
    half, quarter = n // 2, n // 4
    packed[:half, :] = g[:half, :]
    packed[half : half + quarter, :half] = g[half : half + quarter, half:]
    packed[half : half + quarter, half:] = g[half + quarter :, half:]


def unpack_symmetric(packed, g):
    n = g.shape[0]
    half, quarter = n // 2, n // 4
    g[:half, :] = packed[:half, :]
    g[half:, :half] = packed[:half, half:].T
    g[half : half + quarter, half:] = packed[half : half + quarter, :half]
    g[half + quarter :, half:] = packed[half : half + quarter, half:]


def gram_kernel(x, packed):
    pack_symmetric(dot(x[...].T, x[...]), packed)


def begin_first_kernel(scale_first, scale_second, where, own, partner, packed, *refs):
    first_gram, state, over_row, over_col = refs
    gather_rows(where[1], [own, partner], first_gram, first_gram.shape[0] // 2)
    unpack_symmetric(packed, state)
    grams = first_gram[...] * scale_first
    first_gram[...] = grams
    begin_inverse(grams * (state[...] * scale_second), state, over_row, over_col)


def begin_kernel(v, state, over_row, over_col):
    begin_inverse(v[...], state, over_row, over_col)


def begin_second_kernel(scale_second, other, packed, state, over_row, over_col, scaling):
    unpack_symmetric(packed, state)
    raw = state[...] * scale_second
    along_lanes, along_rows = diagonal_of(raw)
    norm_lanes = jnp.sqrt(along_lanes + epsilon)
    norm_rows = jnp.sqrt(along_rows + epsilon)
    scaling[...] = norm_lanes
    begin_inverse(other[...] * (raw / norm_lanes / norm_rows), state, over_row, over_col)


def frames_kernel(scale, scaling, inverse, first_gram, *refs):
    terms, (factor, frame_gram, hadamard) = refs[:-3], refs[-3:]
    frames = factor.shape[0]
    sums = tree([term[...] for term in terms]) / scaling[...]
    raw = dot(sums, inverse[...]) * scale
    norm = jnp.sqrt(jnp.sum(raw * raw, axis=0, keepdims=True) / frames + epsilon)
    normed = raw / norm
    factor[...] = normed
    grams = dot(normed.T, normed) / frames
    frame_gram[...] = grams
    hadamard[...] = first_gram[...] * grams


def second_kernel(where, *refs):
    pieces, (second, packed) = refs[:4], refs[4:]
    gather_rows(where[0], pieces, second, second.shape[0] // QUARTER)
    x = second[...]
    pack_symmetric(dot(x.T, x), packed)


def body(tensor, initial_first, initial_second):
    frames, block_first, block_second = tensor.shape
    rank = initial_first.shape[1]
    square, line, column = (rank, rank), (1, rank), (rank, 1)
    packed = 3 * rank // 4
    part = block_second // QUARTER
    rows_first = block_first * lax.axis_size("row")
    rows_second = block_second * lax.axis_size("col")
    at_x = lax.axis_index("row") // 4
    at_core = lax.axis_index("col") % 2
    where = jnp.stack([at_x, at_core]).astype(jnp.int32)

    (seconds,) = call(gram_kernel, "gram", [(packed, rank)], [VMEM])(initial_second)
    initial_first, seconds = tie(initial_first, seconds)
    seconds = sum_over(seconds, "col", COL_CORE)
    contracted = jnp.einsum("kij,ir->kjr", tensor, initial_first, precision=HIGH)
    terms = jnp.sum(contracted * initial_second[None], axis=1)
    firsts = lax.dynamic_slice_in_dim(gram(initial_first), at_core * (rank // 2), rank // 2)
    both = jnp.concatenate([firsts, terms], 0)
    seconds = sum_over(seconds, "col", COL_Y)
    both = sum_over(both, "row", ROW_X)
    both, seconds = tie(both, seconds)
    seconds = sum_over(seconds, "col", COL_Z)
    both = sum_over(both, "row", ROW_Z)
    firsts, terms = both[: rank // 2], both[rank // 2 :]
    partner = partners(firsts, "col", COL_CORE)[0]
    terms = sum_over(terms, "col", COL_CORE)
    firsts, partner, seconds, terms = tie(firsts, partner, seconds, terms)
    first_gram, state, over_row, over_col = call(
        functools.partial(begin_first_kernel, 1.0 / rows_first, 1.0 / rows_second),
        "begin_first",
        [square, square, line, column],
        [SMEM] + [VMEM] * 3,
        flops=10**6,
    )(where, firsts, partner, seconds)
    terms = sum_over(terms, "col", COL_Y)
    state, terms = tie(state, terms)
    terms = [terms] + partners(terms, "col", COL_Z)
    inverse = finish_inverse(state, over_row, over_col)
    scaling = jnp.ones(line, F32)

    for repeat in range(PASSES):
        factor_frames, frame_gram, hadamard = call(
            functools.partial(frames_kernel, 1.0 / math.sqrt(rows_first * rows_second)),
            "frames",
            [(frames, rank), square, square],
            [VMEM] * (3 + len(terms)),
        )(scaling, inverse, first_gram, *terms)

        sums = jnp.sum(contracted * factor_frames[:, None, :], axis=0)
        own, *sent = [
            lax.dynamic_slice_in_dim(sums, (at_x ^ mask) * part, part) for mask in range(QUARTER)
        ]
        own, *sent, hadamard = tie(own, *sent, hadamard)
        sent = [
            lax.ppermute(piece, "row", [(i, i ^ mask) for i in range(lax.axis_size("row"))])
            for piece, mask in zip(sent, ROW_X)
        ]
        state, over_row, over_col = call(
            begin_kernel, "begin", [square, line, column], [VMEM], flops=10**6
        )(hadamard)
        own, state = tie(tree([own] + sent), state)
        sums = [own] + partners(own, "row", ROW_Z)
        inverse = finish_inverse(state, over_row, over_col)
        *sums, inverse = tie(*sums, inverse)
        piece = dot(tree(sums), inverse) * (1.0 / math.sqrt(rows_first * frames))
        pieces = [piece] + partners(piece, "row", ROW_X)

        last = repeat == PASSES - 1
        second, payload = call(
            second_kernel,
            "second",
            [(block_second, rank), (packed, rank)],
            [SMEM] + [VMEM] * 4,
        )(where, *pieces)
        if not last:
            terms = jnp.sum(contracted * second[None], axis=1)
            payload = jnp.concatenate([payload, terms], 0)
        payload = sum_over(payload, "col", COL_CORE)
        if last:
            terms = jnp.einsum("kij,jr->kir", tensor, second, precision=HIGH)
            terms = jnp.sum(terms * factor_frames[:, None, :], axis=0)
            terms = sum_over(terms, "col", COL_CORE)
            terms = sum_over(terms, "col", COL_Y)
        payload = sum_over(payload, "col", COL_Y)
        payload = sum_over(payload, "col", COL_Z)
        if last:
            other = frame_gram
        else:
            other, payload, terms = first_gram, payload[:packed], payload[packed:]
        payload, terms = tie(payload, terms)
        state, over_row, over_col, scaling = call(
            functools.partial(begin_second_kernel, 1.0 / rows_second),
            "begin_second",
            [square, line, column, line],
            [VMEM] * 2,
            flops=10**6,
        )(other, payload)
        if last:
            terms = sum_over(terms, "col", COL_Z)
        else:
            terms = sum_over(terms, "row", ROW_X)
            state, terms = tie(state, terms)
            terms = [terms] + partners(terms, "row", ROW_Z)
        inverse = finish_inverse(state, over_row, over_col)

    first_raw = dot(terms / scaling, inverse) * (1.0 / math.sqrt(rows_second * frames))
    squares = jnp.sum(first_raw * first_raw, axis=0, keepdims=True)
    squares = sum_over(sum_over(squares, "row", ROW_X), "row", ROW_Z)
    weights = jnp.sqrt(squares[0] / rows_first + epsilon)
    return (first_raw / weights, second / scaling, factor_frames, weights)


def solution(mesh):
    placed = (P(None, "row", "col"), P("row", None), P("col", None))
    return jax.shard_map(
        body,
        mesh=mesh,
        in_specs=placed,
        out_specs=(P("row", None), P("col", None), P(), P()),
        check_vma=False,
    )
```

```python
import functools
import math

import jax
import jax.numpy as jnp
from jax import lax
from jax.experimental import pallas as pl
from jax.experimental.pallas import tpu as pltpu
from jax.sharding import PartitionSpec as P

PASSES = 2
BLOCK = 64
QUARTER = 4

ROW_X = (4, 8, 12)
ROW_Z = (1, 2, 3)
COL_CORE = (1,)
COL_Y = (2, 4, 6)
COL_Z = (8,)

epsilon = 1e-06
HIGHEST = lax.Precision.HIGHEST
HIGH = lax.Precision.HIGH
VMEM = pl.BlockSpec(memory_space=pltpu.VMEM)
ANY = pl.BlockSpec(memory_space=pl.ANY)
SMEM = pl.BlockSpec(memory_space=pltpu.SMEM)
F32 = jnp.float32


def dot(a, b, dims=((1,), (0,))):
    return lax.dot_general(a, b, (dims, ((), ())), precision=HIGHEST, preferred_element_type=F32)


def gram(matrix):
    return dot(matrix, matrix, ((0,), (0,)))


def call(kernel, name, outs, in_specs, scratch=(), keep=None):
    kept = [] if keep is None else [keep]
    run = pl.pallas_call(
        (lambda *refs: kernel(*refs[len(kept) :])),
        scratch_shapes=[pltpu.VMEM(shape, F32) for shape in scratch],
        out_shape=tuple(jax.ShapeDtypeStruct(shape, F32) for shape in outs),
        in_specs=[ANY for array in kept] + in_specs,
        out_specs=tuple(VMEM for shape in outs),
        compiler_params=pltpu.CompilerParams(vmem_limit_bytes=6 << 20),
        name=name,
    )
    return functools.partial(run, *kept)


def partners(x, axis, masks):
    size = lax.axis_size(axis)
    return [lax.ppermute(x, axis, [(i, i ^ mask) for i in range(size)]) for mask in masks]


def tree(terms):
    while len(terms) > 1:
        terms = [terms[i] + terms[i + 1] for i in range(0, len(terms), 2)]
    return terms[0]


def sum_over(x, axis, masks):
    return tree([x] + partners(x, axis, masks))


def tie(*values):
    return lax.optimization_barrier(values)


def invert_pair(a, b, d):
    over = 1.0 / (a * d - b * b)
    return d * over, -b * over, a * over


def invert_small(x, n):
    sub = lax.broadcasted_iota(jnp.int32, (n, n), 0)
    lane = lax.broadcasted_iota(jnp.int32, (n, n), 1)
    lane_row = lax.broadcasted_iota(jnp.int32, (1, n), 1)
    for p in range(0, n, 4):
        c = [jnp.broadcast_to(x[:, p + j : p + j + 1], (n, n)) for j in range(4)]
        a = [[c[j][p + i : p + i + 1, :] for j in range(4)] for i in range(4)]
        inside = (lane_row >= p) & (lane_row < p + 4)
        r = [
            jnp.where(inside, jnp.where(lane_row == p + i, 1.0, 0.0), x[p + i : p + i + 1, :])
            for i in range(4)
        ]
        i00, i01, i11 = invert_pair(a[0][0], a[1][0], a[1][1])
        t20 = a[2][0] * i00 + a[2][1] * i01
        t21 = a[2][0] * i01 + a[2][1] * i11
        t30 = a[3][0] * i00 + a[3][1] * i01
        t31 = a[3][0] * i01 + a[3][1] * i11
        s22 = a[2][2] - (t20 * a[2][0] + t21 * a[2][1])
        s23 = a[3][2] - (t30 * a[2][0] + t31 * a[2][1])
        s33 = a[3][3] - (t30 * a[3][0] + t31 * a[3][1])
        w2 = r[2] - (t20 * r[0] + t21 * r[1])
        w3 = r[3] - (t30 * r[0] + t31 * r[1])
        g0 = i00 * r[0] + i01 * r[1]
        g1 = i01 * r[0] + i11 * r[1]
        j22, j23, j33 = invert_pair(s22, s23, s33)
        q2 = j22 * w2 + j23 * w3
        q3 = j23 * w2 + j33 * w3
        q = [g0 - (t20 * q2 + t30 * q3), g1 - (t21 * q2 + t31 * q3), q2, q3]
        x = jnp.where((lane >= p) & (lane < p + 4), 0.0, x)
        x = x - ((c[0] * q[0] + c[1] * q[1]) + (c[2] * q[2] + c[3] * q[3]))
        for i in range(4):
            x = jnp.where(sub == p + i, q[i], x)
    return x


def eliminate(v, starts):
    n = v.shape[0]
    lane_n = lax.broadcasted_iota(jnp.int32, (n, n), 1)
    lane = lax.broadcasted_iota(jnp.int32, (BLOCK, n), 1)
    sub = lax.broadcasted_iota(jnp.int32, (BLOCK, n), 0)
    for p in starts:
        pivot = invert_small(v[p : p + BLOCK, p : p + BLOCK], BLOCK)
        inside = (lane >= p) & (lane < p + BLOCK)
        rows = jnp.where(inside, jnp.where(lane - p == sub, 1.0, 0.0), v[p : p + BLOCK, :])
        q = dot(pivot, rows)
        cleared = jnp.where((lane_n >= p) & (lane_n < p + BLOCK), 0.0, v)
        rest = cleared - dot(v[:, p : p + BLOCK], q)
        parts = [rest[:p], q, rest[p + BLOCK :]]
        v = jnp.concatenate([part for part in parts if part.shape[0] > 0], 0)
    return v


def diagonal_of(v):
    n = v.shape[0]
    same = lax.broadcasted_iota(jnp.int32, (n, n), 0) == lax.broadcasted_iota(jnp.int32, (n, n), 1)
    kept = jnp.where(same, v, 0.0)
    return jnp.sum(kept, axis=0, keepdims=True), jnp.sum(kept, axis=1, keepdims=True)


def begin_inverse(v, state, over_row, over_col, blocks):
    along_lanes, along_rows = diagonal_of(v)
    over_lanes, over_rows = lax.rsqrt(along_lanes), lax.rsqrt(along_rows)
    over_row[...] = over_lanes
    over_col[...] = over_rows
    state[...] = eliminate(v * over_lanes * over_rows, range(0, blocks * BLOCK, BLOCK))


def middle_kernel(block, state, after):
    after[...] = eliminate(state[...], [block * BLOCK])


def middle_inverse(state, block, keep):
    (after,) = call(
        functools.partial(middle_kernel, block), "middle_inverse", [state.shape], [VMEM], keep=keep
    )(state)
    return after


def finish_kernel(block, state, over_row, over_col, inverse):
    v = eliminate(state[...], range(block * BLOCK, state.shape[0], BLOCK))
    inverse[...] = v * over_row[...] * over_col[...]


def finish_inverse(state, over_row, over_col, block, keep):
    (inverse,) = call(
        functools.partial(finish_kernel, block),
        "finish_inverse",
        [state.shape],
        [VMEM] * 3,
        keep=keep,
    )(state, over_row, over_col)
    return inverse


def gather_rows(position, pieces, into, rows):
    for mask, piece in enumerate(pieces):
        start = pl.multiple_of((position ^ mask) * rows, rows)
        into[pl.ds(start, rows), :] = piece[:rows, :]


def pack_symmetric(g, packed):
    n = g.shape[0]
    half, quarter = n // 2, n // 4
    packed[:half, :] = g[:half, :]
    packed[half : half + quarter, :half] = g[half : half + quarter, half:]
    packed[half : half + quarter, half:] = g[half + quarter :, half:]


def unpack_symmetric(packed, g):
    n = g.shape[0]
    half, quarter = n // 2, n // 4
    g[:half, :] = packed[:half, :]
    g[half:, :half] = packed[:half, half:].T
    g[half : half + quarter, half:] = packed[half : half + quarter, :half]
    g[half + quarter :, half:] = packed[half : half + quarter, half:]


def unpack_pieces(position, pieces, packed, g):
    rows = packed.shape[0] // len(pieces)
    for mask, piece in enumerate(pieces):
        packed[pl.ds(pl.multiple_of((position ^ mask) * rows, rows), rows), :] = piece[:rows, :]
    unpack_symmetric(packed, g)


def grams_kernel(where, first, second, own_first, own_second, packed):
    for at, matrix, own in ((where[1], first, own_first), (where[0], second, own_second)):
        pack_symmetric(dot(matrix[...].T, matrix[...]), packed)
        rows = own.shape[0]
        own[...] = packed[pl.ds(pl.multiple_of(at * rows, rows), rows), :]


def begin_first_kernel(scale_first, scale_second, where, *refs):
    firsts, seconds, (first_gram, state, over_row, over_col, packed) = refs[:2], refs[2:6], refs[6:]
    unpack_pieces(where[1], firsts, packed, first_gram)
    grams = first_gram[...] * scale_first
    first_gram[...] = grams
    unpack_pieces(where[0], seconds, packed, state)
    begin_inverse(grams * (state[...] * scale_second), state, over_row, over_col, 1)


def begin_kernel(v, state, over_row, over_col):
    begin_inverse(v[...], state, over_row, over_col, 2)


def begin_second_kernel(scale_second, where, other, *refs):
    pieces, (state, over_row, over_col, scaling, packed) = refs[:4], refs[4:]
    unpack_pieces(where[0], pieces, packed, state)
    raw = state[...] * scale_second
    along_lanes, along_rows = diagonal_of(raw)
    norm_lanes = jnp.sqrt(along_lanes + epsilon)
    norm_rows = jnp.sqrt(along_rows + epsilon)
    scaling[...] = norm_lanes
    begin_inverse(other[...] * (raw / norm_lanes / norm_rows), state, over_row, over_col, 2)


def frames_kernel(scale, scaling, inverse, first_gram, *refs):
    terms, (factor, frame_gram, hadamard) = refs[:-3], refs[-3:]
    frames = factor.shape[0]
    sums = tree([term[...] for term in terms]) / scaling[...]
    raw = dot(sums, inverse[...]) * scale
    norm = jnp.sqrt(jnp.sum(raw * raw, axis=0, keepdims=True) / frames + epsilon)
    normed = raw / norm
    factor[...] = normed
    grams = dot(normed.T, normed) / frames
    frame_gram[...] = grams
    hadamard[...] = first_gram[...] * grams


def second_kernel(where, *refs):
    pieces, (second, own, packed) = refs[:4], refs[4:]
    gather_rows(where[0], pieces, second, second.shape[0] // QUARTER)
    x = second[...]
    pack_symmetric(dot(x.T, x), packed)
    rows = own.shape[0]
    own[...] = packed[pl.ds(pl.multiple_of(where[0] * rows, rows), rows), :]


def body(tensor, initial_first, initial_second):
    frames, block_first, block_second = tensor.shape
    rank = initial_first.shape[1]
    square, line, column = (rank, rank), (1, rank), (rank, 1)
    packed = (3 * rank // 4, rank)
    half, quarter = packed[0] // 2, packed[0] // 4
    part = block_second // QUARTER
    rows_first = block_first * lax.axis_size("row")
    rows_second = block_second * lax.axis_size("col")
    at_x = lax.axis_index("row") // 4
    at_core = lax.axis_index("col") % 2
    where = jnp.stack([at_x, at_core]).astype(jnp.int32)

    firsts, seconds = call(
        grams_kernel, "grams", [(half, rank), (quarter, rank)], [SMEM] + [VMEM] * 2, [packed]
    )(where, initial_first, initial_second)
    seconds = sum_over(seconds, "col", COL_CORE)
    sent = partners(firsts, "row", ROW_X)
    contracted = jnp.einsum("kij,ir->kjr", tensor, initial_first, precision=HIGH)
    terms = jnp.sum(contracted * initial_second[None], axis=1)
    seconds = sum_over(seconds, "col", COL_Y)
    both = sum_over(jnp.concatenate([tree([firsts] + sent), terms], 0), "row", ROW_Z)
    both, seconds = tie(both, seconds)
    seconds = sum_over(seconds, "col", COL_Z)
    (partner,) = partners(both, "col", COL_CORE)
    both, partner, seconds = tie(both, partner, seconds)
    terms = both[half:] + partner[half:]
    sums = jnp.concatenate([seconds, terms], 0)
    sums = [sums] + partners(sums, "row", ROW_X)
    *sums, terms = tie(*sums, tree([piece[quarter:] for piece in sums]))
    first_gram, state, over_row, over_col = call(
        functools.partial(begin_first_kernel, 1.0 / rows_first, 1.0 / rows_second),
        "begin_first",
        [square, square, line, column],
        [SMEM] + [VMEM] * 6,
        [packed],
        keep=contracted,
    )(where, both, partner, *sums)
    terms = sum_over(terms, "col", COL_Y[:1])
    state, terms = tie(state, terms)
    state = middle_inverse(state, 1, contracted)
    terms = sum_over(terms, "col", COL_Y[1:2])
    state, terms = tie(state, terms)
    terms = [terms] + partners(terms, "col", COL_Z)
    inverse = finish_inverse(state, over_row, over_col, 2, contracted)
    scaling = jnp.ones(line, F32)

    for repeat in range(PASSES):
        last = repeat == PASSES - 1
        keep = None if last else contracted
        factor_frames, frame_gram, hadamard = call(
            functools.partial(frames_kernel, 1.0 / math.sqrt(rows_first * rows_second)),
            "frames",
            [(frames, rank), square, square],
            [VMEM] * (3 + len(terms)),
        )(scaling, inverse, first_gram, *terms)

        sums = jnp.sum(contracted * factor_frames[:, None, :], axis=0)
        own, *sent = [
            lax.dynamic_slice_in_dim(sums, (at_x ^ mask) * part, part) for mask in range(QUARTER)
        ]
        own, *sent, hadamard = tie(own, *sent, hadamard)
        sent = [
            lax.ppermute(piece, "row", [(i, i ^ mask) for i in range(lax.axis_size("row"))])
            for piece, mask in zip(sent, ROW_X)
        ]
        state, over_row, over_col = call(
            begin_kernel, "begin", [square, line, column], [VMEM], keep=keep
        )(hadamard)
        own, state = tie(tree([own] + sent), state)
        sums = [own] + partners(own, "row", ROW_Z)
        inverse = finish_inverse(state, over_row, over_col, 2, keep)
        *sums, inverse = tie(*sums, inverse)
        piece = dot(tree(sums), inverse) * (1.0 / math.sqrt(rows_first * frames))
        pieces = [piece] + partners(piece, "row", ROW_X)

        second, payload = call(
            second_kernel,
            "second",
            [(block_second, rank), (quarter, rank)],
            [SMEM] + [VMEM] * 4,
            [packed],
        )(where, *pieces)
        if not last:
            terms = jnp.sum(contracted * second[None], axis=1)
            payload = jnp.concatenate([payload, terms], 0)
        payload = sum_over(payload, "col", COL_CORE)
        payload = sum_over(payload, "col", COL_Y)
        if last:
            payload, later = tie(payload, second)
            terms = jnp.einsum("kij,jr->kir", tensor, later, precision=HIGH)
            terms = jnp.sum(terms * factor_frames[:, None, :], axis=0)
            terms = sum_over(terms, "col", COL_CORE)
        payload = sum_over(payload, "col", COL_Z)
        if last:
            payload, terms = tie(payload, terms)
            terms = sum_over(terms, "col", COL_Y[:1])
        sums = [payload] + partners(payload, "row", ROW_X)
        if not last:
            terms = tree([piece[quarter:] for piece in sums])
        *sums, terms = tie(*sums, terms)
        state, over_row, over_col, scaling = call(
            functools.partial(begin_second_kernel, 1.0 / rows_second),
            "begin_second",
            [square, line, column, line],
            [SMEM] + [VMEM] * 5,
            [packed],
            keep=keep,
        )(where, frame_gram if last else first_gram, *sums)
        if last:
            terms = sum_over(terms, "col", COL_Y[1:2])
            state, terms = tie(state, terms)
            terms = sum_over(terms, "col", COL_Z)
        else:
            terms = sum_over(terms, "row", ROW_Z[:1])
            state, terms = tie(state, terms)
            terms = [terms] + partners(terms, "row", ROW_Z[1:2])
        inverse = finish_inverse(state, over_row, over_col, 2, keep)

    first_raw = dot(terms / scaling, inverse) * (1.0 / math.sqrt(rows_second * frames))
    squares = jnp.sum(first_raw * first_raw, axis=0, keepdims=True)
    squares = sum_over(sum_over(squares, "row", ROW_X), "row", ROW_Z)
    weights = jnp.sqrt(squares[0] / rows_first + epsilon)
    return (first_raw / weights, second / scaling, factor_frames, weights)


def solution(mesh):
    placed = (P(None, "row", "col"), P("row", None), P("col", None))
    return jax.shard_map(
        body,
        mesh=mesh,
        in_specs=placed,
        out_specs=(P("row", None), P("col", None), P(), P()),
        check_vma=False,
    )
```

```python
import functools
import math

import jax
import jax.numpy as jnp
from jax import lax
from jax.experimental import pallas as pl
from jax.experimental.pallas import tpu as pltpu
from jax.sharding import PartitionSpec as P

PASSES = 2
BLOCK = 64
QUARTER = 4

ROW_X = (4, 8, 12)
ROW_Z = (1, 2, 3)
COL_CORE = (1,)
COL_Y = (2, 4, 6)
COL_Z = (8,)

epsilon = 1e-06
HIGHEST = lax.Precision.HIGHEST
HIGH = lax.Precision.HIGH
VMEM = pl.BlockSpec(memory_space=pltpu.VMEM)
ANY = pl.BlockSpec(memory_space=pl.ANY)
SMEM = pl.BlockSpec(memory_space=pltpu.SMEM)
F32 = jnp.float32


def dot(a, b, dims=((1,), (0,))):
    return lax.dot_general(a, b, (dims, ((), ())), precision=HIGHEST, preferred_element_type=F32)


def gram(matrix):
    return dot(matrix, matrix, ((0,), (0,)))


def call(kernel, name, outs, in_specs, scratch=(), keep=None):
    kept = [] if keep is None else [keep]
    run = pl.pallas_call(
        (lambda *refs: kernel(*refs[len(kept) :])),
        scratch_shapes=[pltpu.VMEM(shape, F32) for shape in scratch],
        out_shape=tuple(jax.ShapeDtypeStruct(shape, F32) for shape in outs),
        in_specs=[ANY for array in kept] + in_specs,
        out_specs=tuple(VMEM for shape in outs),
        compiler_params=pltpu.CompilerParams(vmem_limit_bytes=6 << 20),
        name=name,
    )
    return functools.partial(run, *kept)


def partners(x, axis, masks):
    size = lax.axis_size(axis)
    return [lax.ppermute(x, axis, [(i, i ^ mask) for i in range(size)]) for mask in masks]


def tree(terms):
    while len(terms) > 1:
        terms = [terms[i] + terms[i + 1] for i in range(0, len(terms), 2)]
    return terms[0]


def sum_over(x, axis, masks):
    return tree([x] + partners(x, axis, masks))


def tie(*values):
    return lax.optimization_barrier(values)


def sum_kernel(*refs):
    refs[-1][...] = tree([ref[...] for ref in refs[:-1]])


def sum_keeping(x, axis, masks, keep):
    terms = [x] + partners(x, axis, masks)
    (total,) = call(sum_kernel, "sum", [x.shape], [VMEM] * len(terms), keep=keep)(*terms)
    return total


def split_kernel(*refs):
    pieces, (top, bottom) = refs[:-2], refs[-2:]
    top[...] = tree([piece[: top.shape[0], :] for piece in pieces])
    bottom[...] = tree([piece[piece.shape[0] - bottom.shape[0] :, :] for piece in pieces])


def invert_four(a):
    det = a[0][0] * a[1][1] - a[1][0] * a[1][0]
    u20 = a[2][0] * a[1][1] - a[2][1] * a[1][0]
    u21 = a[2][1] * a[0][0] - a[2][0] * a[1][0]
    u30 = a[3][0] * a[1][1] - a[3][1] * a[1][0]
    u31 = a[3][1] * a[0][0] - a[3][0] * a[1][0]
    s22 = det * a[2][2] - (u20 * a[2][0] + u21 * a[2][1])
    s32 = det * a[3][2] - (u30 * a[2][0] + u31 * a[2][1])
    s33 = det * a[3][3] - (u30 * a[3][0] + u31 * a[3][1])
    over = 1.0 / det
    scale = det / (s22 * s33 - s32 * s32)
    j22, j32, j33 = s33 * scale, -s32 * scale, s22 * scale
    t20, t21, t30, t31 = u20 * over, u21 * over, u30 * over, u31 * over
    p20, p21 = -(j22 * t20 + j32 * t30), -(j22 * t21 + j32 * t31)
    p30, p31 = -(j32 * t20 + j33 * t30), -(j32 * t21 + j33 * t31)
    p00 = a[1][1] * over - (t20 * p20 + t30 * p30)
    p10 = -a[1][0] * over - (t21 * p20 + t31 * p30)
    p11 = a[0][0] * over - (t21 * p21 + t31 * p31)
    return [[p00, p10, p20, p30], [p10, p11, p21, p31], [p20, p21, j22, j32], [p30, p31, j32, j33]]


def combine(weights, terms):
    return (weights[0] * terms[0] + weights[1] * terms[1]) + (
        weights[2] * terms[2] + weights[3] * terms[3]
    )


def invert_small(x, n):
    tiles = n // 8
    x = [x[8 * k : 8 * k + 8, :] for k in range(tiles)]
    lane = lax.broadcasted_iota(jnp.int32, (8, n), 1)
    sub = lax.broadcasted_iota(jnp.int32, (8, n), 0)

    def spread(tile, row):
        return jnp.broadcast_to(tile[row : row + 1, :], (8, n))

    def columns(p):
        return [
            [jnp.broadcast_to(tile[:, p + j : p + j + 1], (8, n)) for tile in x] for j in range(4)
        ]

    def updated(old, rows, k, at, first):
        new = old - combine([now[j][k] for j in range(4)], rows)
        if k == at:
            for i in range(4):
                new = jnp.where(sub == first + i, rows[i], new)
        return new

    now = columns(0)
    for p in range(0, n, 4):
        at, first = p // 8, p % 8
        ahead = columns(p + 4) if p + 4 < n else None
        pivot = invert_four([[spread(now[j][at], first + i) for j in range(i + 1)] for i in range(4)])
        inside = (lane >= p) & (lane < p + 4)
        rows = [
            jnp.where(inside, jnp.where(lane == p + i, 1.0, 0.0), spread(x[at], first + i))
            for i in range(4)
        ]
        if ahead is not None:
            at_next, first_next = (p + 4) // 8, (p + 4) % 8
            later = []
            for j in range(4):
                entries = [spread(now[i][at_next], first_next + j) for i in range(4)]
                entries = [combine(pivot[i], entries) for i in range(4)]
                later.append([updated(ahead[j][k], entries, k, at, first) for k in range(tiles)])
        rows = [combine(pivot[i], rows) for i in range(4)]
        x = [updated(jnp.where(inside, 0.0, x[k]), rows, k, at, first) for k in range(tiles)]
        if ahead is not None:
            now = later
    return jnp.concatenate(x, 0)


def eliminate(v, starts):
    n = v.shape[0]
    lane_n = lax.broadcasted_iota(jnp.int32, (n, n), 1)
    lane = lax.broadcasted_iota(jnp.int32, (BLOCK, n), 1)
    sub = lax.broadcasted_iota(jnp.int32, (BLOCK, n), 0)
    for p in starts:
        pivot = invert_small(v[p : p + BLOCK, p : p + BLOCK], BLOCK)
        inside = (lane >= p) & (lane < p + BLOCK)
        rows = jnp.where(inside, jnp.where(lane - p == sub, 1.0, 0.0), v[p : p + BLOCK, :])
        q = dot(pivot, rows)
        cleared = jnp.where((lane_n >= p) & (lane_n < p + BLOCK), 0.0, v)
        rest = cleared - dot(v[:, p : p + BLOCK], q)
        parts = [rest[:p], q, rest[p + BLOCK :]]
        v = jnp.concatenate([part for part in parts if part.shape[0] > 0], 0)
    return v


def diagonal_of(v):
    n = v.shape[0]
    same = lax.broadcasted_iota(jnp.int32, (n, n), 0) == lax.broadcasted_iota(jnp.int32, (n, n), 1)
    kept = jnp.where(same, v, 0.0)
    return jnp.sum(kept, axis=0, keepdims=True), jnp.sum(kept, axis=1, keepdims=True)


def begin_inverse(v, state, over_row, over_col):
    along_lanes, along_rows = diagonal_of(v)
    over_lanes, over_rows = lax.rsqrt(along_lanes), lax.rsqrt(along_rows)
    over_row[...] = over_lanes
    over_col[...] = over_rows
    state[...] = eliminate(v * over_lanes * over_rows, range(0, 2 * BLOCK, BLOCK))


def finish_kernel(state, over_row, over_col, inverse):
    v = eliminate(state[...], range(2 * BLOCK, state.shape[0], BLOCK))
    inverse[...] = v * over_row[...] * over_col[...]


def finish_inverse(state, over_row, over_col, keep):
    (inverse,) = call(
        finish_kernel,
        "finish_inverse",
        [state.shape],
        [VMEM] * 3,
        keep=keep,
    )(state, over_row, over_col)
    return inverse


def gather_rows(position, pieces, into, rows):
    for mask, piece in enumerate(pieces):
        start = pl.multiple_of((position ^ mask) * rows, rows)
        into[pl.ds(start, rows), :] = piece[:rows, :]


def pack_symmetric(g, packed):
    n = g.shape[0]
    half, quarter = n // 2, n // 4
    packed[:half, :] = g[:half, :]
    packed[half : half + quarter, :half] = g[half : half + quarter, half:]
    packed[half : half + quarter, half:] = g[half + quarter :, half:]


def unpack_symmetric(packed, g):
    n = g.shape[0]
    half, quarter = n // 2, n // 4
    g[:half, :] = packed[:half, :]
    g[half:, :half] = packed[:half, half:].T
    g[half : half + quarter, half:] = packed[half : half + quarter, :half]
    g[half + quarter :, half:] = packed[half : half + quarter, half:]


def unpack_pieces(position, pieces, packed, g, skip=0):
    rows = packed.shape[0] // len(pieces)
    for mask, piece in enumerate(pieces):
        start = pl.multiple_of((position ^ mask) * rows, rows)
        packed[pl.ds(start, rows), :] = piece[skip : skip + rows, :]
    unpack_symmetric(packed, g)


def grams_kernel(where, first, second, own_first, own_second, packed):
    for at, matrix, own in ((where[1], first, own_first), (where[0], second, own_second)):
        pack_symmetric(dot(matrix[...].T, matrix[...]), packed)
        rows = own.shape[0]
        own[...] = packed[pl.ds(pl.multiple_of(at * rows, rows), rows), :]


def begin_first_kernel(scale_first, scale_second, where, *refs):
    firsts, seconds, (first_gram, state, over_row, over_col, packed) = refs[:2], refs[2:6], refs[6:]
    unpack_pieces(where[1], firsts, packed, first_gram)
    grams = first_gram[...] * scale_first
    first_gram[...] = grams
    unpack_pieces(where[0], seconds, packed, state, firsts[0].shape[0])
    begin_inverse(grams * (state[...] * scale_second), state, over_row, over_col)


def begin_kernel(v, state, over_row, over_col):
    begin_inverse(v[...], state, over_row, over_col)


def begin_second_kernel(scale_second, where, other, *refs):
    pieces, (state, over_row, over_col, scaling, packed) = refs[:4], refs[4:]
    unpack_pieces(where[0], pieces, packed, state)
    raw = state[...] * scale_second
    along_lanes, along_rows = diagonal_of(raw)
    norm_lanes = jnp.sqrt(along_lanes + epsilon)
    norm_rows = jnp.sqrt(along_rows + epsilon)
    scaling[...] = norm_lanes
    begin_inverse(other[...] * (raw / norm_lanes / norm_rows), state, over_row, over_col)


def frames_kernel(scale, scaling, inverse, first_gram, *refs):
    terms, (factor, frame_gram, hadamard) = refs[:-3], refs[-3:]
    frames = factor.shape[0]
    sums = tree([term[...] for term in terms]) / scaling[...]
    raw = dot(sums, inverse[...]) * scale
    norm = jnp.sqrt(jnp.sum(raw * raw, axis=0, keepdims=True) / frames + epsilon)
    normed = raw / norm
    factor[...] = normed
    grams = dot(normed.T, normed) / frames
    frame_gram[...] = grams
    hadamard[...] = first_gram[...] * grams


def second_kernel(where, *refs):
    pieces, (second, own, packed) = refs[:4], refs[4:]
    gather_rows(where[0], pieces, second, second.shape[0] // QUARTER)
    x = second[...]
    pack_symmetric(dot(x.T, x), packed)
    rows = own.shape[0]
    own[...] = packed[pl.ds(pl.multiple_of(where[0] * rows, rows), rows), :]


def body(tensor, initial_first, initial_second):
    frames, block_first, block_second = tensor.shape
    rank = initial_first.shape[1]
    square, line, column = (rank, rank), (1, rank), (rank, 1)
    packed = (3 * rank // 4, rank)
    half, quarter = packed[0] // 2, packed[0] // 4
    part = block_second // QUARTER
    rows_first = block_first * lax.axis_size("row")
    rows_second = block_second * lax.axis_size("col")
    at_x = lax.axis_index("row") // 4
    at_core = lax.axis_index("col") % 2
    where = jnp.stack([at_x, at_core]).astype(jnp.int32)

    firsts, seconds = call(
        grams_kernel, "grams", [(half, rank), (quarter, rank)], [SMEM] + [VMEM] * 2, [packed]
    )(where, initial_first, initial_second)
    contracted = jnp.einsum("kij,ir->kjr", tensor, initial_first, precision=HIGH)
    terms = jnp.sum(contracted * initial_second[None], axis=1)
    firsts = sum_keeping(jnp.concatenate([firsts, terms], 0), "row", ROW_Z, contracted)
    seconds = jnp.concatenate([seconds, firsts[half:]], 0)
    seconds = sum_over(seconds, "col", COL_CORE)
    seconds = sum_keeping(seconds, "col", COL_Y, contracted)
    seconds = sum_over(seconds, "col", COL_Z)
    pieces = jnp.concatenate([firsts[:half], seconds], 0)
    pieces = [pieces] + partners(pieces, "row", ROW_X)
    firsts, terms = call(
        split_kernel, "split", [(half, rank), (frames, rank)], [VMEM] * 4, keep=contracted
    )(*pieces)
    (partner,) = partners(firsts, "col", COL_CORE)
    first_gram, state, over_row, over_col = call(
        functools.partial(begin_first_kernel, 1.0 / rows_first, 1.0 / rows_second),
        "begin_first",
        [square, square, line, column],
        [SMEM] + [VMEM] * 6,
        [packed],
    )(where, firsts, partner, *pieces)
    inverse = finish_inverse(state, over_row, over_col, None)
    terms = [terms]
    scaling = jnp.ones(line, F32)

    for repeat in range(PASSES):
        last = repeat == PASSES - 1
        keep = None if last else contracted
        factor_frames, frame_gram, hadamard = call(
            functools.partial(frames_kernel, 1.0 / math.sqrt(rows_first * rows_second)),
            "frames",
            [(frames, rank), square, square],
            [VMEM] * (3 + len(terms)),
        )(scaling, inverse, first_gram, *terms)

        sums = jnp.sum(contracted * factor_frames[:, None, :], axis=0)
        own, *sent = [
            lax.dynamic_slice_in_dim(sums, (at_x ^ mask) * part, part) for mask in range(QUARTER)
        ]
        own, *sent, hadamard = tie(own, *sent, hadamard)
        sent = [
            lax.ppermute(piece, "row", [(i, i ^ mask) for i in range(lax.axis_size("row"))])
            for piece, mask in zip(sent, ROW_X)
        ]
        state, over_row, over_col = call(
            begin_kernel, "begin", [square, line, column], [VMEM], keep=keep
        )(hadamard)
        own, state = tie(tree([own] + sent), state)
        sums = [own] + partners(own, "row", ROW_Z)
        inverse = finish_inverse(state, over_row, over_col, keep)
        *sums, inverse = tie(*sums, inverse)
        piece = dot(tree(sums), inverse) * (1.0 / math.sqrt(rows_first * frames))
        pieces = [piece] + partners(piece, "row", ROW_X)

        second, payload = call(
            second_kernel,
            "second",
            [(block_second, rank), (quarter, rank)],
            [SMEM] + [VMEM] * 4,
            [packed],
        )(where, *pieces)
        if not last:
            terms = jnp.sum(contracted * second[None], axis=1)
            payload = jnp.concatenate([payload, terms], 0)
        payload = sum_over(payload, "col", COL_CORE)
        payload = sum_over(payload, "col", COL_Y)
        payload = sum_over(payload, "col", COL_Z)
        if last:
            terms = jnp.einsum("kij,jr->kir", tensor, second, precision=HIGH)
            terms = jnp.sum(terms * factor_frames[:, None, :], axis=0)
            for masks in (COL_CORE, COL_Y, COL_Z):
                terms = sum_over(terms, "col", masks)
        sums = [payload] + partners(payload, "row", ROW_X)
        if not last:
            terms = tree([piece[quarter:] for piece in sums])
            *sums, terms = tie(*sums, terms)
        state, over_row, over_col, scaling = call(
            functools.partial(begin_second_kernel, 1.0 / rows_second),
            "begin_second",
            [square, line, column, line],
            [SMEM] + [VMEM] * 5,
            [packed],
            keep=keep,
        )(where, frame_gram if last else first_gram, *sums)
        if not last:
            terms = sum_over(terms, "row", ROW_Z[:1])
            state, terms = tie(state, terms)
            terms = [terms] + partners(terms, "row", ROW_Z[1:2])
        inverse = finish_inverse(state, over_row, over_col, keep)

    first_raw = dot(terms / scaling, inverse) * (1.0 / math.sqrt(rows_second * frames))
    squares = jnp.sum(first_raw * first_raw, axis=0, keepdims=True)
    squares = sum_over(sum_over(squares, "row", ROW_X), "row", ROW_Z)
    weights = jnp.sqrt(squares[0] / rows_first + epsilon)
    return (first_raw / weights, second / scaling, factor_frames, weights)


def solution(mesh):
    placed = (P(None, "row", "col"), P("row", None), P("col", None))
    return jax.shard_map(
        body,
        mesh=mesh,
        in_specs=placed,
        out_specs=(P("row", None), P("col", None), P(), P()),
        check_vma=False,
    )
```

```python
import functools
import math

import jax
import jax.numpy as jnp
from jax import lax
from jax.experimental import pallas as pl
from jax.experimental.pallas import tpu as pltpu
from jax.sharding import PartitionSpec as P

PASSES = 2
BLOCK = 64
QUARTER = 4

ROW_X = (4, 8, 12)
ROW_Z = (1, 2, 3)
COL_CORE = (1,)
COL_Y = (2, 4, 6)
COL_Z = (8,)

epsilon = 1e-06
HIGHEST = lax.Precision.HIGHEST
HIGH = lax.Precision.HIGH
VMEM = pl.BlockSpec(memory_space=pltpu.VMEM)
ANY = pl.BlockSpec(memory_space=pl.ANY)
SMEM = pl.BlockSpec(memory_space=pltpu.SMEM)
F32 = jnp.float32


def dot(a, b, dims=((1,), (0,))):
    return lax.dot_general(a, b, (dims, ((), ())), precision=HIGHEST, preferred_element_type=F32)


def gram(matrix):
    return dot(matrix, matrix, ((0,), (0,)))


def call(kernel, name, outs, in_specs, scratch=(), keep=None):
    kept = [] if keep is None else [keep]
    run = pl.pallas_call(
        (lambda *refs: kernel(*refs[len(kept) :])),
        scratch_shapes=[pltpu.VMEM(shape, F32) for shape in scratch],
        out_shape=tuple(jax.ShapeDtypeStruct(shape, F32) for shape in outs),
        in_specs=[ANY for array in kept] + in_specs,
        out_specs=tuple(VMEM for shape in outs),
        compiler_params=pltpu.CompilerParams(vmem_limit_bytes=6 << 20),
        name=name,
    )
    return functools.partial(run, *kept)


def partners(x, axis, masks):
    size = lax.axis_size(axis)
    return [lax.ppermute(x, axis, [(i, i ^ mask) for i in range(size)]) for mask in masks]


def tree(terms):
    while len(terms) > 1:
        terms = [terms[i] + terms[i + 1] for i in range(0, len(terms), 2)]
    return terms[0]


def sum_over(x, axis, masks):
    return tree([x] + partners(x, axis, masks))


def tie(*values):
    return lax.optimization_barrier(values)


def sum_kernel(*refs):
    refs[-1][...] = tree([ref[...] for ref in refs[:-1]])


def sum_keeping(x, axis, masks, keep):
    terms = [x] + partners(x, axis, masks)
    (total,) = call(sum_kernel, "sum", [x.shape], [VMEM] * len(terms), keep=keep)(*terms)
    return total


def cross_kernel(where, *refs):
    pieces, (total, gathered) = refs[:-2], refs[-2:]
    top, rows = total.shape[0], gathered.shape[0] // len(pieces)
    total[...] = tree([piece[:top, :] for piece in pieces])
    for mask, piece in enumerate(pieces):
        start = pl.multiple_of((where[2] ^ mask) * rows, rows)
        gathered[pl.ds(start, rows), :] = piece[top:, :]


def split_kernel(*refs):
    pieces, (top, bottom) = refs[:-2], refs[-2:]
    top[...] = tree([piece[: top.shape[0], :] for piece in pieces])
    bottom[...] = tree([piece[piece.shape[0] - bottom.shape[0] :, :] for piece in pieces])


def invert_four(a):
    det = a[0][0] * a[1][1] - a[1][0] * a[1][0]
    u20 = a[2][0] * a[1][1] - a[2][1] * a[1][0]
    u21 = a[2][1] * a[0][0] - a[2][0] * a[1][0]
    u30 = a[3][0] * a[1][1] - a[3][1] * a[1][0]
    u31 = a[3][1] * a[0][0] - a[3][0] * a[1][0]
    s22 = det * a[2][2] - (u20 * a[2][0] + u21 * a[2][1])
    s32 = det * a[3][2] - (u30 * a[2][0] + u31 * a[2][1])
    s33 = det * a[3][3] - (u30 * a[3][0] + u31 * a[3][1])
    over = 1.0 / det
    scale = det / (s22 * s33 - s32 * s32)
    j22, j32, j33 = s33 * scale, -s32 * scale, s22 * scale
    t20, t21, t30, t31 = u20 * over, u21 * over, u30 * over, u31 * over
    p20, p21 = -(j22 * t20 + j32 * t30), -(j22 * t21 + j32 * t31)
    p30, p31 = -(j32 * t20 + j33 * t30), -(j32 * t21 + j33 * t31)
    p00 = a[1][1] * over - (t20 * p20 + t30 * p30)
    p10 = -a[1][0] * over - (t21 * p20 + t31 * p30)
    p11 = a[0][0] * over - (t21 * p21 + t31 * p31)
    return [[p00, p10, p20, p30], [p10, p11, p21, p31], [p20, p21, j22, j32], [p30, p31, j32, j33]]


def combine(weights, terms):
    return (weights[0] * terms[0] + weights[1] * terms[1]) + (
        weights[2] * terms[2] + weights[3] * terms[3]
    )


def invert_small(x, n):
    tiles = n // 8
    x = [x[8 * k : 8 * k + 8, :] for k in range(tiles)]
    lane = lax.broadcasted_iota(jnp.int32, (8, n), 1)
    sub = lax.broadcasted_iota(jnp.int32, (8, n), 0)

    def spread(tile, row):
        return jnp.broadcast_to(tile[row : row + 1, :], (8, n))

    def columns(p):
        return [
            [jnp.broadcast_to(tile[:, p + j : p + j + 1], (8, n)) for tile in x] for j in range(4)
        ]

    def updated(old, rows, k, at, first):
        new = old - combine([now[j][k] for j in range(4)], rows)
        if k == at:
            for i in range(4):
                new = jnp.where(sub == first + i, rows[i], new)
        return new

    now = columns(0)
    for p in range(0, n, 4):
        at, first = p // 8, p % 8
        ahead = columns(p + 4) if p + 4 < n else None
        pivot = invert_four([[spread(now[j][at], first + i) for j in range(i + 1)] for i in range(4)])
        inside = (lane >= p) & (lane < p + 4)
        rows = [
            jnp.where(inside, jnp.where(lane == p + i, 1.0, 0.0), spread(x[at], first + i))
            for i in range(4)
        ]
        if ahead is not None:
            at_next, first_next = (p + 4) // 8, (p + 4) % 8
            later = []
            for j in range(4):
                entries = [spread(now[i][at_next], first_next + j) for i in range(4)]
                entries = [combine(pivot[i], entries) for i in range(4)]
                later.append([updated(ahead[j][k], entries, k, at, first) for k in range(tiles)])
        rows = [combine(pivot[i], rows) for i in range(4)]
        x = [updated(jnp.where(inside, 0.0, x[k]), rows, k, at, first) for k in range(tiles)]
        if ahead is not None:
            now = later
    return jnp.concatenate(x, 0)


def eliminate(v, starts):
    n = v.shape[0]
    lane_n = lax.broadcasted_iota(jnp.int32, (n, n), 1)
    lane = lax.broadcasted_iota(jnp.int32, (BLOCK, n), 1)
    sub = lax.broadcasted_iota(jnp.int32, (BLOCK, n), 0)
    for p in starts:
        pivot = invert_small(v[p : p + BLOCK, p : p + BLOCK], BLOCK)
        inside = (lane >= p) & (lane < p + BLOCK)
        rows = jnp.where(inside, jnp.where(lane - p == sub, 1.0, 0.0), v[p : p + BLOCK, :])
        q = dot(pivot, rows)
        cleared = jnp.where((lane_n >= p) & (lane_n < p + BLOCK), 0.0, v)
        rest = cleared - dot(v[:, p : p + BLOCK], q)
        parts = [rest[:p], q, rest[p + BLOCK :]]
        v = jnp.concatenate([part for part in parts if part.shape[0] > 0], 0)
    return v


def diagonal_of(v):
    n = v.shape[0]
    same = lax.broadcasted_iota(jnp.int32, (n, n), 0) == lax.broadcasted_iota(jnp.int32, (n, n), 1)
    kept = jnp.where(same, v, 0.0)
    return jnp.sum(kept, axis=0, keepdims=True), jnp.sum(kept, axis=1, keepdims=True)


def begin_inverse(v, state, over_row, over_col, blocks=2):
    along_lanes, along_rows = diagonal_of(v)
    over_lanes, over_rows = lax.rsqrt(along_lanes), lax.rsqrt(along_rows)
    over_row[...] = over_lanes
    over_col[...] = over_rows
    state[...] = eliminate(v * over_lanes * over_rows, range(0, blocks * BLOCK, BLOCK))


def finish_kernel(state, over_row, over_col, inverse):
    v = eliminate(state[...], range(2 * BLOCK, state.shape[0], BLOCK))
    inverse[...] = v * over_row[...] * over_col[...]


def finish_inverse(state, over_row, over_col, keep):
    (inverse,) = call(
        finish_kernel,
        "finish_inverse",
        [state.shape],
        [VMEM] * 3,
        keep=keep,
    )(state, over_row, over_col)
    return inverse


def gather_rows(position, pieces, into, rows):
    for mask, piece in enumerate(pieces):
        start = pl.multiple_of((position ^ mask) * rows, rows)
        into[pl.ds(start, rows), :] = piece[:rows, :]


def pack_symmetric(g, packed):
    n = g.shape[0]
    half, quarter = n // 2, n // 4
    packed[:half, :] = g[:half, :]
    packed[half : half + quarter, :half] = g[half : half + quarter, half:]
    packed[half : half + quarter, half:] = g[half + quarter :, half:]


def unpack_symmetric(packed, g):
    n = g.shape[0]
    half, quarter = n // 2, n // 4
    g[:half, :] = packed[:half, :]
    g[half:, :half] = packed[:half, half:].T
    g[half : half + quarter, half:] = packed[half : half + quarter, :half]
    g[half + quarter :, half:] = packed[half : half + quarter, half:]


def unpack_pieces(position, pieces, packed, g, skip=0):
    rows = packed.shape[0] // len(pieces)
    for mask, piece in enumerate(pieces):
        start = pl.multiple_of((position ^ mask) * rows, rows)
        packed[pl.ds(start, rows), :] = piece[skip : skip + rows, :]
    unpack_symmetric(packed, g)


def grams_kernel(where, first, second, own_first, own_second, packed):
    position = where[1] * QUARTER + where[2]
    for at, matrix, own in ((position, first, own_first), (where[0], second, own_second)):
        pack_symmetric(dot(matrix[...].T, matrix[...]), packed)
        rows = own.shape[0]
        own[...] = packed[pl.ds(pl.multiple_of(at * rows, rows), rows), :]


def begin_first_kernel(scale_first, scale_second, where, *refs):
    firsts, seconds, (first_gram, state, over_row, over_col, packed) = refs[:2], refs[2:6], refs[6:]
    unpack_pieces(where[1], firsts, packed, first_gram)
    grams = first_gram[...] * scale_first
    first_gram[...] = grams
    unpack_pieces(where[0], seconds, packed, state, firsts[0].shape[0])
    begin_inverse(grams * (state[...] * scale_second), state, over_row, over_col)


def begin_kernel(v, state, over_row, over_col):
    begin_inverse(v[...], state, over_row, over_col, 1)


def middle_kernel(state, after):
    after[...] = eliminate(state[...], [BLOCK])


def begin_second_kernel(scale_second, where, other, *refs):
    pieces, (state, over_row, over_col, scaling, packed) = refs[:4], refs[4:]
    unpack_pieces(where[0], pieces, packed, state)
    raw = state[...] * scale_second
    along_lanes, along_rows = diagonal_of(raw)
    norm_lanes = jnp.sqrt(along_lanes + epsilon)
    norm_rows = jnp.sqrt(along_rows + epsilon)
    scaling[...] = norm_lanes
    begin_inverse(other[...] * (raw / norm_lanes / norm_rows), state, over_row, over_col)


def frames_kernel(scale, scaling, inverse, first_gram, *refs):
    terms, (factor, frame_gram, hadamard) = refs[:-3], refs[-3:]
    frames = factor.shape[0]
    sums = tree([term[...] for term in terms]) / scaling[...]
    raw = dot(sums, inverse[...]) * scale
    norm = jnp.sqrt(jnp.sum(raw * raw, axis=0, keepdims=True) / frames + epsilon)
    normed = raw / norm
    factor[...] = normed
    grams = dot(normed.T, normed) / frames
    frame_gram[...] = grams
    hadamard[...] = first_gram[...] * grams


def second_kernel(scale, where, inverse, *refs):
    pieces, (second, own, packed) = refs[:4], refs[4:]
    gather_rows(where[0], pieces, second, second.shape[0] // QUARTER)
    x = dot(second[...], inverse[...]) * scale
    second[...] = x
    pack_symmetric(dot(x.T, x), packed)
    rows = own.shape[0]
    own[...] = packed[pl.ds(pl.multiple_of(where[0] * rows, rows), rows), :]


def body(tensor, initial_first, initial_second):
    frames, block_first, block_second = tensor.shape
    rank = initial_first.shape[1]
    square, line, column = (rank, rank), (1, rank), (rank, 1)
    packed = (3 * rank // 4, rank)
    half, quarter, eighth = packed[0] // 2, packed[0] // 4, packed[0] // 8
    part = block_second // QUARTER
    rows_first = block_first * lax.axis_size("row")
    rows_second = block_second * lax.axis_size("col")
    at_x = lax.axis_index("row") // 4
    at_core = lax.axis_index("col") % 2
    at_y = lax.axis_index("col") // 2 % QUARTER
    where = jnp.stack([at_x, at_core, at_y]).astype(jnp.int32)

    firsts, seconds = call(
        grams_kernel, "grams", [(eighth, rank), (quarter, rank)], [SMEM] + [VMEM] * 2, [packed]
    )(where, initial_first, initial_second)
    contracted = jnp.einsum("kij,ir->kjr", tensor, initial_first, precision=HIGH)
    terms = jnp.sum(contracted * initial_second[None], axis=1)
    firsts = sum_keeping(jnp.concatenate([firsts, terms], 0), "row", ROW_Z, contracted)
    seconds = jnp.concatenate([seconds, firsts[eighth:]], 0)
    seconds = sum_over(seconds, "col", COL_CORE)
    pieces = jnp.concatenate([seconds, firsts[:eighth]], 0)
    pieces = [pieces] + partners(pieces, "col", COL_Y)
    seconds, firsts = call(
        cross_kernel,
        "cross",
        [seconds.shape, (half, rank)],
        [SMEM] + [VMEM] * 4,
        keep=contracted,
    )(where, *pieces)
    seconds = sum_over(seconds, "col", COL_Z)
    pieces = jnp.concatenate([firsts, seconds], 0)
    pieces = [pieces] + partners(pieces, "row", ROW_X)
    firsts, terms = call(
        split_kernel, "split", [(half, rank), (frames, rank)], [VMEM] * 4, keep=contracted
    )(*pieces)
    (partner,) = partners(firsts, "col", COL_CORE)
    first_gram, state, over_row, over_col = call(
        functools.partial(begin_first_kernel, 1.0 / rows_first, 1.0 / rows_second),
        "begin_first",
        [square, square, line, column],
        [SMEM] + [VMEM] * 6,
        [packed],
    )(where, firsts, partner, *pieces)
    inverse = finish_inverse(state, over_row, over_col, None)
    terms = [terms]
    scaling = jnp.ones(line, F32)

    for repeat in range(PASSES):
        last = repeat == PASSES - 1
        keep = None if last else contracted
        factor_frames, frame_gram, hadamard = call(
            functools.partial(frames_kernel, 1.0 / math.sqrt(rows_first * rows_second)),
            "frames",
            [(frames, rank), square, square],
            [VMEM] * (3 + len(terms)),
        )(scaling, inverse, first_gram, *terms)

        sums = jnp.sum(contracted * factor_frames[:, None, :], axis=0)
        own, *sent = [
            lax.dynamic_slice_in_dim(sums, (at_x ^ mask) * part, part) for mask in range(QUARTER)
        ]
        own, *sent, hadamard = tie(own, *sent, hadamard)
        sent = [
            lax.ppermute(piece, "row", [(i, i ^ mask) for i in range(lax.axis_size("row"))])
            for piece, mask in zip(sent, ROW_X)
        ]
        state, over_row, over_col = call(
            begin_kernel, "begin", [square, line, column], [VMEM], keep=keep
        )(hadamard)
        own, state = tie(tree([own] + sent), state)
        sums = [own] + partners(own, "row", ROW_Z)
        (state,) = call(middle_kernel, "middle", [square], [VMEM], keep=keep)(state)
        *sums, state = tie(*sums, state)
        piece = tree(sums)
        pieces = [piece] + partners(piece, "row", ROW_X)
        inverse = finish_inverse(state, over_row, over_col, keep)

        second, payload = call(
            functools.partial(second_kernel, 1.0 / math.sqrt(rows_first * frames)),
            "second",
            [(block_second, rank), (quarter, rank)],
            [SMEM] + [VMEM] * 5,
            [packed],
        )(where, inverse, *pieces)
        if not last:
            terms = jnp.sum(contracted * second[None], axis=1)
            payload = jnp.concatenate([payload, terms], 0)
        payload = sum_over(payload, "col", COL_CORE)
        payload = sum_over(payload, "col", COL_Y)
        if last:
            terms = jnp.einsum("kij,jr->kir", tensor, second, precision=HIGH)
            terms = jnp.sum(terms * factor_frames[:, None, :], axis=0)
            terms = sum_over(terms, "col", COL_CORE)
            payload, terms = tie(payload, terms)
            terms = sum_over(terms, "col", COL_Y[:1])
        payload = sum_over(payload, "col", COL_Z)
        if last:
            payload, terms = tie(payload, terms)
            terms = sum_over(terms, "col", COL_Y[1:2])
        sums = [payload] + partners(payload, "row", ROW_X)
        if not last:
            terms = tree([piece[quarter:] for piece in sums])
        *sums, terms = tie(*sums, terms)
        if last:
            terms = sum_over(terms, "col", COL_Z)
        state, over_row, over_col, scaling = call(
            functools.partial(begin_second_kernel, 1.0 / rows_second),
            "begin_second",
            [square, line, column, line],
            [SMEM] + [VMEM] * 5,
            [packed],
            keep=keep,
        )(where, frame_gram if last else first_gram, *sums)
        if not last:
            terms = sum_over(terms, "row", ROW_Z[:1])
            state, terms = tie(state, terms)
            terms = [terms] + partners(terms, "row", ROW_Z[1:2])
        inverse = finish_inverse(state, over_row, over_col, keep)

    first_raw = dot(terms / scaling, inverse) * (1.0 / math.sqrt(rows_second * frames))
    squares = jnp.sum(first_raw * first_raw, axis=0, keepdims=True)
    squares = sum_over(sum_over(squares, "row", ROW_X), "row", ROW_Z)
    weights = jnp.sqrt(squares[0] / rows_first + epsilon)
    return (first_raw / weights, second / scaling, factor_frames, weights)


def solution(mesh):
    placed = (P(None, "row", "col"), P("row", None), P("col", None))
    return jax.shard_map(
        body,
        mesh=mesh,
        in_specs=placed,
        out_specs=(P("row", None), P("col", None), P(), P()),
        check_vma=False,
    )
```

```python
import functools
import math

import jax
import jax.numpy as jnp
from jax import lax
from jax.experimental import pallas as pl
from jax.experimental.pallas import tpu as pltpu
from jax.sharding import PartitionSpec as P

PASSES = 2
BLOCK = 64
QUARTER = 4

ROW_X = (4, 8, 12)
ROW_Z = (1, 2, 3)
COL_CORE = (1,)
COL_Y = (2, 4, 6)
COL_Z = (8,)

epsilon = 1e-06
HIGHEST = lax.Precision.HIGHEST
HIGH = lax.Precision.HIGH
VMEM = pl.BlockSpec(memory_space=pltpu.VMEM)
ANY = pl.BlockSpec(memory_space=pl.ANY)
SMEM = pl.BlockSpec(memory_space=pltpu.SMEM)
F32 = jnp.float32


def dot(a, b, dims=((1,), (0,))):
    return lax.dot_general(a, b, (dims, ((), ())), precision=HIGHEST, preferred_element_type=F32)


def gram(matrix):
    return dot(matrix, matrix, ((0,), (0,)))


def call(kernel, name, outs, in_specs, scratch=(), keep=None):
    kept = [] if keep is None else [keep]
    run = pl.pallas_call(
        (lambda *refs: kernel(*refs[len(kept) :])),
        scratch_shapes=[pltpu.VMEM(shape, F32) for shape in scratch],
        out_shape=tuple(jax.ShapeDtypeStruct(shape, F32) for shape in outs),
        in_specs=[ANY for array in kept] + in_specs,
        out_specs=tuple(VMEM for shape in outs),
        compiler_params=pltpu.CompilerParams(vmem_limit_bytes=6 << 20),
        name=name,
    )
    return functools.partial(run, *kept)


def partners(x, axis, masks):
    size = lax.axis_size(axis)
    return [lax.ppermute(x, axis, [(i, i ^ mask) for i in range(size)]) for mask in masks]


def tree(terms):
    while len(terms) > 1:
        terms = [terms[i] + terms[i + 1] for i in range(0, len(terms), 2)]
    return terms[0]


def sum_over(x, axis, masks):
    return tree([x] + partners(x, axis, masks))


def tie(*values):
    return lax.optimization_barrier(values)


def sum_kernel(*refs):
    refs[-1][...] = tree([ref[...] for ref in refs[:-1]])


def sum_keeping(x, axis, masks, keep):
    terms = [x] + partners(x, axis, masks)
    (total,) = call(sum_kernel, "sum", [x.shape], [VMEM] * len(terms), keep=keep)(*terms)
    return total


def cross_kernel(where, *refs):
    pieces, (total, gathered) = refs[:-2], refs[-2:]
    top, rows = total.shape[0], gathered.shape[0] // len(pieces)
    total[...] = tree([piece[:top, :] for piece in pieces])
    for mask, piece in enumerate(pieces):
        start = pl.multiple_of((where[2] ^ mask) * rows, rows)
        gathered[pl.ds(start, rows), :] = piece[top:, :]


def split_kernel(*refs):
    pieces, (top, bottom) = refs[:-2], refs[-2:]
    top[...] = tree([piece[: top.shape[0], :] for piece in pieces])
    bottom[...] = tree([piece[piece.shape[0] - bottom.shape[0] :, :] for piece in pieces])


def invert_four(a):
    det = a[0][0] * a[1][1] - a[1][0] * a[1][0]
    u20 = a[2][0] * a[1][1] - a[2][1] * a[1][0]
    u21 = a[2][1] * a[0][0] - a[2][0] * a[1][0]
    u30 = a[3][0] * a[1][1] - a[3][1] * a[1][0]
    u31 = a[3][1] * a[0][0] - a[3][0] * a[1][0]
    s22 = det * a[2][2] - (u20 * a[2][0] + u21 * a[2][1])
    s32 = det * a[3][2] - (u30 * a[2][0] + u31 * a[2][1])
    s33 = det * a[3][3] - (u30 * a[3][0] + u31 * a[3][1])
    over = 1.0 / det
    scale = det / (s22 * s33 - s32 * s32)
    j22, j32, j33 = s33 * scale, -s32 * scale, s22 * scale
    t20, t21, t30, t31 = u20 * over, u21 * over, u30 * over, u31 * over
    p20, p21 = -(j22 * t20 + j32 * t30), -(j22 * t21 + j32 * t31)
    p30, p31 = -(j32 * t20 + j33 * t30), -(j32 * t21 + j33 * t31)
    p00 = a[1][1] * over - (t20 * p20 + t30 * p30)
    p10 = -a[1][0] * over - (t21 * p20 + t31 * p30)
    p11 = a[0][0] * over - (t21 * p21 + t31 * p31)
    return [[p00, p10, p20, p30], [p10, p11, p21, p31], [p20, p21, j22, j32], [p30, p31, j32, j33]]


def combine(weights, terms):
    return (weights[0] * terms[0] + weights[1] * terms[1]) + (
        weights[2] * terms[2] + weights[3] * terms[3]
    )


def invert_small(x, n):
    tiles = n // 8
    x = [x[8 * k : 8 * k + 8, :] for k in range(tiles)]
    lane = lax.broadcasted_iota(jnp.int32, (8, n), 1)
    sub = lax.broadcasted_iota(jnp.int32, (8, n), 0)

    def spread(tile, row):
        return jnp.broadcast_to(tile[row : row + 1, :], (8, n))

    def columns(p):
        return [
            [jnp.broadcast_to(tile[:, p + j : p + j + 1], (8, n)) for tile in x] for j in range(4)
        ]

    def updated(old, rows, k, at, first):
        new = old - combine([now[j][k] for j in range(4)], rows)
        if k == at:
            for i in range(4):
                new = jnp.where(sub == first + i, rows[i], new)
        return new

    now = columns(0)
    for p in range(0, n, 4):
        at, first = p // 8, p % 8
        ahead = columns(p + 4) if p + 4 < n else None
        pivot = invert_four([[spread(now[j][at], first + i) for j in range(i + 1)] for i in range(4)])
        inside = (lane >= p) & (lane < p + 4)
        rows = [
            jnp.where(inside, jnp.where(lane == p + i, 1.0, 0.0), spread(x[at], first + i))
            for i in range(4)
        ]
        if ahead is not None:
            at_next, first_next = (p + 4) // 8, (p + 4) % 8
            later = []
            for j in range(4):
                entries = [spread(now[i][at_next], first_next + j) for i in range(4)]
                entries = [combine(pivot[i], entries) for i in range(4)]
                later.append([updated(ahead[j][k], entries, k, at, first) for k in range(tiles)])
        rows = [combine(pivot[i], rows) for i in range(4)]
        x = [updated(jnp.where(inside, 0.0, x[k]), rows, k, at, first) for k in range(tiles)]
        if ahead is not None:
            now = later
    return jnp.concatenate(x, 0)


def eliminate(v, starts):
    n = v.shape[0]
    lane_n = lax.broadcasted_iota(jnp.int32, (n, n), 1)
    lane = lax.broadcasted_iota(jnp.int32, (BLOCK, n), 1)
    sub = lax.broadcasted_iota(jnp.int32, (BLOCK, n), 0)
    for p in starts:
        pivot = invert_small(v[p : p + BLOCK, p : p + BLOCK], BLOCK)
        inside = (lane >= p) & (lane < p + BLOCK)
        rows = jnp.where(inside, jnp.where(lane - p == sub, 1.0, 0.0), v[p : p + BLOCK, :])
        q = dot(pivot, rows)
        cleared = jnp.where((lane_n >= p) & (lane_n < p + BLOCK), 0.0, v)
        rest = cleared - dot(v[:, p : p + BLOCK], q)
        parts = [rest[:p], q, rest[p + BLOCK :]]
        v = jnp.concatenate([part for part in parts if part.shape[0] > 0], 0)
    return v


def diagonal_of(v):
    n = v.shape[0]
    same = lax.broadcasted_iota(jnp.int32, (n, n), 0) == lax.broadcasted_iota(jnp.int32, (n, n), 1)
    kept = jnp.where(same, v, 0.0)
    return jnp.sum(kept, axis=0, keepdims=True), jnp.sum(kept, axis=1, keepdims=True)


def begin_inverse(v, state, over_row, over_col, blocks=2):
    along_lanes, along_rows = diagonal_of(v)
    over_lanes, over_rows = lax.rsqrt(along_lanes), lax.rsqrt(along_rows)
    over_row[...] = over_lanes
    over_col[...] = over_rows
    state[...] = eliminate(v * over_lanes * over_rows, range(0, blocks * BLOCK, BLOCK))


def finish_kernel(state, over_row, over_col, inverse):
    v = eliminate(state[...], range(2 * BLOCK, state.shape[0], BLOCK))
    inverse[...] = v * over_row[...] * over_col[...]


def finish_inverse(state, over_row, over_col, keep):
    (inverse,) = call(
        finish_kernel,
        "finish_inverse",
        [state.shape],
        [VMEM] * 3,
        keep=keep,
    )(state, over_row, over_col)
    return inverse


def gather_rows(position, pieces, into, rows):
    for mask, piece in enumerate(pieces):
        start = pl.multiple_of((position ^ mask) * rows, rows)
        into[pl.ds(start, rows), :] = piece[:rows, :]


def pack_symmetric(g, packed):
    n = g.shape[0]
    half, quarter = n // 2, n // 4
    packed[:half, :] = g[:half, :]
    packed[half : half + quarter, :half] = g[half : half + quarter, half:]
    packed[half : half + quarter, half:] = g[half + quarter :, half:]


def unpack_symmetric(packed, g):
    n = g.shape[0]
    half, quarter = n // 2, n // 4
    g[:half, :] = packed[:half, :]
    g[half:, :half] = packed[:half, half:].T
    g[half : half + quarter, half:] = packed[half : half + quarter, :half]
    g[half + quarter :, half:] = packed[half : half + quarter, half:]


def unpack_pieces(position, pieces, packed, g, skip=0):
    rows = packed.shape[0] // len(pieces)
    for mask, piece in enumerate(pieces):
        start = pl.multiple_of((position ^ mask) * rows, rows)
        packed[pl.ds(start, rows), :] = piece[skip : skip + rows, :]
    unpack_symmetric(packed, g)


def grams_kernel(where, first, second, own_first, own_second, packed):
    position = where[1] * QUARTER + where[2]
    for at, matrix, own in ((position, first, own_first), (where[0], second, own_second)):
        pack_symmetric(dot(matrix[...].T, matrix[...]), packed)
        rows = own.shape[0]
        own[...] = packed[pl.ds(pl.multiple_of(at * rows, rows), rows), :]


def begin_first_kernel(scale_first, scale_second, where, *refs):
    firsts, seconds, (first_gram, state, over_row, over_col, packed) = refs[:2], refs[2:6], refs[6:]
    unpack_pieces(where[1], firsts, packed, first_gram)
    grams = first_gram[...] * scale_first
    first_gram[...] = grams
    unpack_pieces(where[0], seconds, packed, state, firsts[0].shape[0])
    begin_inverse(grams * (state[...] * scale_second), state, over_row, over_col)


def begin_kernel(v, state, over_row, over_col):
    begin_inverse(v[...], state, over_row, over_col, 1)


def middle_kernel(state, after):
    after[...] = eliminate(state[...], [BLOCK])


def begin_second_kernel(scale_second, where, other, *refs):
    pieces, (state, over_row, over_col, scaling, packed) = refs[:4], refs[4:]
    unpack_pieces(where[0], pieces, packed, state)
    raw = state[...] * scale_second
    along_lanes, along_rows = diagonal_of(raw)
    norm_lanes = jnp.sqrt(along_lanes + epsilon)
    norm_rows = jnp.sqrt(along_rows + epsilon)
    scaling[...] = norm_lanes
    begin_inverse(other[...] * (raw / norm_lanes / norm_rows), state, over_row, over_col)


def frames_kernel(scale, where, scaling, inverse, first_gram, contracted, *refs):
    terms, (factor, frame_gram, hadamard), quarters = refs[:-7], refs[-7:-4], refs[-4:]
    frames = factor.shape[0]
    sums = tree([term[...] for term in terms]) / scaling[...]
    raw = dot(sums, inverse[...]) * scale
    norm = jnp.sqrt(jnp.sum(raw * raw, axis=0, keepdims=True) / frames + epsilon)
    normed = raw / norm
    factor[...] = normed
    grams = dot(normed.T, normed) / frames
    frame_gram[...] = grams
    hadamard[...] = first_gram[...] * grams
    for mask, quarter in enumerate(quarters):
        rows = quarter.shape[0]
        start = pl.multiple_of((where[0] ^ mask) * rows, rows)
        total = contracted[0, pl.ds(start, rows), :] * normed[0:1, :]
        for k in range(1, frames):
            total = total + contracted[k, pl.ds(start, rows), :] * normed[k : k + 1, :]
        quarter[...] = total


def second_kernel(scale, where, inverse, *refs):
    pieces, (second, own, packed) = refs[:4], refs[4:]
    gather_rows(where[0], pieces, second, second.shape[0] // QUARTER)
    x = dot(second[...], inverse[...]) * scale
    second[...] = x
    pack_symmetric(dot(x.T, x), packed)
    rows = own.shape[0]
    own[...] = packed[pl.ds(pl.multiple_of(where[0] * rows, rows), rows), :]


def body(tensor, initial_first, initial_second):
    frames, block_first, block_second = tensor.shape
    rank = initial_first.shape[1]
    square, line, column = (rank, rank), (1, rank), (rank, 1)
    packed = (3 * rank // 4, rank)
    half, quarter, eighth = packed[0] // 2, packed[0] // 4, packed[0] // 8
    part = block_second // QUARTER
    rows_first = block_first * lax.axis_size("row")
    rows_second = block_second * lax.axis_size("col")
    at_x = lax.axis_index("row") // 4
    at_core = lax.axis_index("col") % 2
    at_y = lax.axis_index("col") // 2 % QUARTER
    where = jnp.stack([at_x, at_core, at_y]).astype(jnp.int32)

    firsts, seconds = call(
        grams_kernel, "grams", [(eighth, rank), (quarter, rank)], [SMEM] + [VMEM] * 2, [packed]
    )(where, initial_first, initial_second)
    contracted = jnp.einsum("kij,ir->kjr", tensor, initial_first, precision=HIGH)
    terms = jnp.sum(contracted * initial_second[None], axis=1)
    firsts = sum_keeping(jnp.concatenate([firsts, terms], 0), "row", ROW_Z, contracted)
    seconds = jnp.concatenate([seconds, firsts[eighth:]], 0)
    seconds = sum_over(seconds, "col", COL_CORE)
    pieces = jnp.concatenate([seconds, firsts[:eighth]], 0)
    pieces = [pieces] + partners(pieces, "col", COL_Y)
    seconds, firsts = call(
        cross_kernel,
        "cross",
        [seconds.shape, (half, rank)],
        [SMEM] + [VMEM] * 4,
        keep=contracted,
    )(where, *pieces)
    seconds = sum_over(seconds, "col", COL_Z)
    pieces = jnp.concatenate([firsts, seconds], 0)
    pieces = [pieces] + partners(pieces, "row", ROW_X)
    firsts, terms = call(
        split_kernel, "split", [(half, rank), (frames, rank)], [VMEM] * 4, keep=contracted
    )(*pieces)
    (partner,) = partners(firsts, "col", COL_CORE)
    first_gram, state, over_row, over_col = call(
        functools.partial(begin_first_kernel, 1.0 / rows_first, 1.0 / rows_second),
        "begin_first",
        [square, square, line, column],
        [SMEM] + [VMEM] * 6,
        [packed],
    )(where, firsts, partner, *pieces)
    inverse = finish_inverse(state, over_row, over_col, None)
    terms = [terms]
    scaling = jnp.ones(line, F32)

    for repeat in range(PASSES):
        last = repeat == PASSES - 1
        keep = None if last else contracted
        factor_frames, frame_gram, hadamard, own, *sent = call(
            functools.partial(frames_kernel, 1.0 / math.sqrt(rows_first * rows_second)),
            "frames",
            [(frames, rank), square, square] + [(part, rank)] * QUARTER,
            [SMEM] + [VMEM] * (4 + len(terms)),
        )(where, scaling, inverse, first_gram, contracted, *terms)
        sent = [
            lax.ppermute(piece, "row", [(i, i ^ mask) for i in range(lax.axis_size("row"))])
            for piece, mask in zip(sent, ROW_X)
        ]
        state, over_row, over_col = call(
            begin_kernel, "begin", [square, line, column], [VMEM], keep=keep
        )(hadamard)
        own, state = tie(tree([own] + sent), state)
        sums = [own] + partners(own, "row", ROW_Z)
        (state,) = call(middle_kernel, "middle", [square], [VMEM], keep=keep)(state)
        *sums, state = tie(*sums, state)
        piece = tree(sums)
        pieces = [piece] + partners(piece, "row", ROW_X)
        inverse = finish_inverse(state, over_row, over_col, keep)

        second, payload = call(
            functools.partial(second_kernel, 1.0 / math.sqrt(rows_first * frames)),
            "second",
            [(block_second, rank), (quarter, rank)],
            [SMEM] + [VMEM] * 5,
            [packed],
        )(where, inverse, *pieces)
        if not last:
            terms = jnp.sum(contracted * second[None], axis=1)
            payload = jnp.concatenate([payload, terms], 0)
        payload = sum_over(payload, "col", COL_CORE)
        payload = sum_over(payload, "col", COL_Y)
        if last:
            terms = jnp.einsum("kij,jr->kir", tensor, second, precision=HIGH)
            terms = jnp.sum(terms * factor_frames[:, None, :], axis=0)
            terms = sum_over(terms, "col", COL_CORE)
            payload, terms = tie(payload, terms)
            terms = sum_over(terms, "col", COL_Y[:1])
        payload = sum_over(payload, "col", COL_Z)
        if last:
            payload, terms = tie(payload, terms)
            terms = sum_over(terms, "col", COL_Y[1:2])
        sums = [payload] + partners(payload, "row", ROW_X)
        if not last:
            terms = tree([piece[quarter:] for piece in sums])
        *sums, terms = tie(*sums, terms)
        if last:
            terms = sum_over(terms, "col", COL_Z)
        state, over_row, over_col, scaling = call(
            functools.partial(begin_second_kernel, 1.0 / rows_second),
            "begin_second",
            [square, line, column, line],
            [SMEM] + [VMEM] * 5,
            [packed],
            keep=keep,
        )(where, frame_gram if last else first_gram, *sums)
        if not last:
            terms = sum_over(terms, "row", ROW_Z[:1])
            state, terms = tie(state, terms)
            terms = [terms] + partners(terms, "row", ROW_Z[1:2])
        inverse = finish_inverse(state, over_row, over_col, keep)

    first_raw = dot(terms / scaling, inverse) * (1.0 / math.sqrt(rows_second * frames))
    squares = jnp.sum(first_raw * first_raw, axis=0, keepdims=True)
    squares = sum_over(sum_over(squares, "row", ROW_X), "row", ROW_Z)
    weights = jnp.sqrt(squares[0] / rows_first + epsilon)
    return (first_raw / weights, second / scaling, factor_frames, weights)


def solution(mesh):
    placed = (P(None, "row", "col"), P("row", None), P("col", None))
    return jax.shard_map(
        body,
        mesh=mesh,
        in_specs=placed,
        out_specs=(P("row", None), P("col", None), P(), P()),
        check_vma=False,
    )
```

```python
import functools
import math

import jax
import jax.numpy as jnp
from jax import lax
from jax.experimental import pallas as pl
from jax.experimental.pallas import tpu as pltpu
from jax.sharding import PartitionSpec as P

PASSES = 2
BLOCK = 64
QUARTER = 4

ROW_X = (4, 8, 12)
ROW_Z = (1, 2, 3)
COL_CORE = (1,)
COL_Y = (2, 4, 6)
COL_Z = (8,)

epsilon = 1e-06
HIGHEST = lax.Precision.HIGHEST
HIGH = lax.Precision.HIGH
VMEM = pl.BlockSpec(memory_space=pltpu.VMEM)
ANY = pl.BlockSpec(memory_space=pl.ANY)
SMEM = pl.BlockSpec(memory_space=pltpu.SMEM)
F32 = jnp.float32


def dot(a, b, dims=((1,), (0,))):
    return lax.dot_general(a, b, (dims, ((), ())), precision=HIGHEST, preferred_element_type=F32)


def gram(matrix):
    return dot(matrix, matrix, ((0,), (0,)))


def call(kernel, name, outs, in_specs, scratch=(), keep=None):
    kept = [] if keep is None else [keep]
    run = pl.pallas_call(
        (lambda *refs: kernel(*refs[len(kept) :])),
        scratch_shapes=[pltpu.VMEM(shape, F32) for shape in scratch],
        out_shape=tuple(jax.ShapeDtypeStruct(shape, F32) for shape in outs),
        in_specs=[ANY for array in kept] + in_specs,
        out_specs=tuple(VMEM for shape in outs),
        compiler_params=pltpu.CompilerParams(vmem_limit_bytes=6 << 20),
        name=name,
    )
    return functools.partial(run, *kept)


def partners(x, axis, masks):
    size = lax.axis_size(axis)
    return [lax.ppermute(x, axis, [(i, i ^ mask) for i in range(size)]) for mask in masks]


def tree(terms):
    while len(terms) > 1:
        terms = [terms[i] + terms[i + 1] for i in range(0, len(terms), 2)]
    return terms[0]


def sum_over(x, axis, masks):
    return tree([x] + partners(x, axis, masks))


def tie(*values):
    return lax.optimization_barrier(values)


def sum_kernel(*refs):
    refs[-1][...] = tree([ref[...] for ref in refs[:-1]])


def sum_keeping(x, axis, masks, keep):
    terms = [x] + partners(x, axis, masks)
    (total,) = call(sum_kernel, "sum", [x.shape], [VMEM] * len(terms), keep=keep)(*terms)
    return total


def cross_kernel(where, *refs):
    pieces, (total, gathered) = refs[:-2], refs[-2:]
    top, rows = total.shape[0], gathered.shape[0] // len(pieces)
    total[...] = tree([piece[:top, :] for piece in pieces])
    for mask, piece in enumerate(pieces):
        start = pl.multiple_of((where[2] ^ mask) * rows, rows)
        gathered[pl.ds(start, rows), :] = piece[top:, :]


def split_kernel(*refs):
    pieces, (top, bottom) = refs[:-2], refs[-2:]
    top[...] = tree([piece[: top.shape[0], :] for piece in pieces])
    bottom[...] = tree([piece[piece.shape[0] - bottom.shape[0] :, :] for piece in pieces])


def invert_four(a):
    det = a[0][0] * a[1][1] - a[1][0] * a[1][0]
    u20 = a[2][0] * a[1][1] - a[2][1] * a[1][0]
    u21 = a[2][1] * a[0][0] - a[2][0] * a[1][0]
    u30 = a[3][0] * a[1][1] - a[3][1] * a[1][0]
    u31 = a[3][1] * a[0][0] - a[3][0] * a[1][0]
    s22 = det * a[2][2] - (u20 * a[2][0] + u21 * a[2][1])
    s32 = det * a[3][2] - (u30 * a[2][0] + u31 * a[2][1])
    s33 = det * a[3][3] - (u30 * a[3][0] + u31 * a[3][1])
    over = 1.0 / det
    scale = det / (s22 * s33 - s32 * s32)
    j22, j32, j33 = s33 * scale, -s32 * scale, s22 * scale
    t20, t21, t30, t31 = u20 * over, u21 * over, u30 * over, u31 * over
    p20, p21 = -(j22 * t20 + j32 * t30), -(j22 * t21 + j32 * t31)
    p30, p31 = -(j32 * t20 + j33 * t30), -(j32 * t21 + j33 * t31)
    p00 = a[1][1] * over - (t20 * p20 + t30 * p30)
    p10 = -a[1][0] * over - (t21 * p20 + t31 * p30)
    p11 = a[0][0] * over - (t21 * p21 + t31 * p31)
    return [[p00, p10, p20, p30], [p10, p11, p21, p31], [p20, p21, j22, j32], [p30, p31, j32, j33]]


def combine(weights, terms):
    return (weights[0] * terms[0] + weights[1] * terms[1]) + (
        weights[2] * terms[2] + weights[3] * terms[3]
    )


def invert_small(x, n):
    tiles = n // 8
    x = [x[8 * k : 8 * k + 8, :] for k in range(tiles)]
    lane = lax.broadcasted_iota(jnp.int32, (8, n), 1)
    sub = lax.broadcasted_iota(jnp.int32, (8, n), 0)

    def spread(tile, row):
        return jnp.broadcast_to(tile[row : row + 1, :], (8, n))

    def columns(p):
        return [
            [jnp.broadcast_to(tile[:, p + j : p + j + 1], (8, n)) for tile in x] for j in range(4)
        ]

    def updated(old, rows, k, at, first):
        new = old - combine([now[j][k] for j in range(4)], rows)
        if k == at:
            for i in range(4):
                new = jnp.where(sub == first + i, rows[i], new)
        return new

    now = columns(0)
    for p in range(0, n, 4):
        at, first = p // 8, p % 8
        ahead = columns(p + 4) if p + 4 < n else None
        pivot = invert_four([[spread(now[j][at], first + i) for j in range(i + 1)] for i in range(4)])
        inside = (lane >= p) & (lane < p + 4)
        rows = [
            jnp.where(inside, jnp.where(lane == p + i, 1.0, 0.0), spread(x[at], first + i))
            for i in range(4)
        ]
        if ahead is not None:
            at_next, first_next = (p + 4) // 8, (p + 4) % 8
            later = []
            for j in range(4):
                entries = [spread(now[i][at_next], first_next + j) for i in range(4)]
                entries = [combine(pivot[i], entries) for i in range(4)]
                later.append([updated(ahead[j][k], entries, k, at, first) for k in range(tiles)])
        rows = [combine(pivot[i], rows) for i in range(4)]
        x = [updated(jnp.where(inside, 0.0, x[k]), rows, k, at, first) for k in range(tiles)]
        if ahead is not None:
            now = later
    return jnp.concatenate(x, 0)


def eliminate(v, starts):
    n = v.shape[0]
    lane_n = lax.broadcasted_iota(jnp.int32, (n, n), 1)
    lane = lax.broadcasted_iota(jnp.int32, (BLOCK, n), 1)
    sub = lax.broadcasted_iota(jnp.int32, (BLOCK, n), 0)
    for p in starts:
        pivot = invert_small(v[p : p + BLOCK, p : p + BLOCK], BLOCK)
        inside = (lane >= p) & (lane < p + BLOCK)
        rows = jnp.where(inside, jnp.where(lane - p == sub, 1.0, 0.0), v[p : p + BLOCK, :])
        q = dot(pivot, rows)
        cleared = jnp.where((lane_n >= p) & (lane_n < p + BLOCK), 0.0, v)
        rest = cleared - dot(v[:, p : p + BLOCK], q)
        parts = [rest[:p], q, rest[p + BLOCK :]]
        v = jnp.concatenate([part for part in parts if part.shape[0] > 0], 0)
    return v


def diagonal_of(v):
    n = v.shape[0]
    same = lax.broadcasted_iota(jnp.int32, (n, n), 0) == lax.broadcasted_iota(jnp.int32, (n, n), 1)
    kept = jnp.where(same, v, 0.0)
    return jnp.sum(kept, axis=0, keepdims=True), jnp.sum(kept, axis=1, keepdims=True)


def begin_inverse(v, state, over_row, over_col, blocks=2):
    along_lanes, along_rows = diagonal_of(v)
    over_lanes, over_rows = lax.rsqrt(along_lanes), lax.rsqrt(along_rows)
    over_row[...] = over_lanes
    over_col[...] = over_rows
    state[...] = eliminate(v * over_lanes * over_rows, range(0, blocks * BLOCK, BLOCK))


def finish_kernel(state, over_row, over_col, inverse):
    v = eliminate(state[...], range(2 * BLOCK, state.shape[0], BLOCK))
    inverse[...] = v * over_row[...] * over_col[...]


def finish_inverse(state, over_row, over_col, keep):
    (inverse,) = call(
        finish_kernel,
        "finish_inverse",
        [state.shape],
        [VMEM] * 3,
        keep=keep,
    )(state, over_row, over_col)
    return inverse


def gather_rows(position, pieces, into, rows):
    for mask, piece in enumerate(pieces):
        start = pl.multiple_of((position ^ mask) * rows, rows)
        into[pl.ds(start, rows), :] = piece[:rows, :]


def pack_symmetric(g, packed):
    n = g.shape[0]
    half, quarter = n // 2, n // 4
    packed[:half, :] = g[:half, :]
    packed[half : half + quarter, :half] = g[half : half + quarter, half:]
    packed[half : half + quarter, half:] = g[half + quarter :, half:]


def unpack_symmetric(packed, g):
    n = g.shape[0]
    half, quarter = n // 2, n // 4
    g[:half, :] = packed[:half, :]
    g[half:, :half] = packed[:half, half:].T
    g[half : half + quarter, half:] = packed[half : half + quarter, :half]
    g[half + quarter :, half:] = packed[half : half + quarter, half:]


def unpack_pieces(position, pieces, packed, g, skip=0):
    rows = packed.shape[0] // len(pieces)
    for mask, piece in enumerate(pieces):
        start = pl.multiple_of((position ^ mask) * rows, rows)
        packed[pl.ds(start, rows), :] = piece[skip : skip + rows, :]
    unpack_symmetric(packed, g)


def grams_kernel(where, first, second, own_first, own_second, packed):
    position = where[1] * QUARTER + where[2]
    for at, matrix, own in ((position, first, own_first), (where[0], second, own_second)):
        pack_symmetric(dot(matrix[...].T, matrix[...]), packed)
        rows = own.shape[0]
        own[...] = packed[pl.ds(pl.multiple_of(at * rows, rows), rows), :]


def begin_first_kernel(scale_first, scale_second, where, *refs):
    firsts, seconds, (first_gram, state, over_row, over_col, packed) = refs[:2], refs[2:6], refs[6:]
    unpack_pieces(where[1], firsts, packed, first_gram)
    grams = first_gram[...] * scale_first
    first_gram[...] = grams
    unpack_pieces(where[0], seconds, packed, state, firsts[0].shape[0])
    begin_inverse(grams * (state[...] * scale_second), state, over_row, over_col)


def begin_kernel(v, state, over_row, over_col):
    begin_inverse(v[...], state, over_row, over_col, 1)


def middle_kernel(state, after):
    after[...] = eliminate(state[...], [BLOCK])


def begin_second_kernel(scale_second, where, other, *refs):
    pieces, (state, over_row, over_col, scaling, packed) = refs[:4], refs[4:]
    unpack_pieces(where[0], pieces, packed, state)
    raw = state[...] * scale_second
    along_lanes, along_rows = diagonal_of(raw)
    norm_lanes = jnp.sqrt(along_lanes + epsilon)
    norm_rows = jnp.sqrt(along_rows + epsilon)
    scaling[...] = norm_lanes
    begin_inverse(other[...] * (raw / norm_lanes / norm_rows), state, over_row, over_col)


def frames_kernel(scale, where, scaling, inverse, first_gram, contracted, *refs):
    terms, (factor, frame_gram, hadamard), quarters = refs[:-7], refs[-7:-4], refs[-4:]
    frames = factor.shape[0]
    sums = tree([term[...] for term in terms]) / scaling[...]
    raw = dot(sums, inverse[...]) * scale
    norm = jnp.sqrt(jnp.sum(raw * raw, axis=0, keepdims=True) / frames + epsilon)
    normed = raw / norm
    factor[...] = normed
    grams = dot(normed.T, normed) / frames
    frame_gram[...] = grams
    hadamard[...] = first_gram[...] * grams
    for mask, quarter in enumerate(quarters):
        rows = quarter.shape[0]
        start = pl.multiple_of((where[0] ^ mask) * rows, rows)
        total = contracted[0, pl.ds(start, rows), :] * normed[0:1, :]
        for k in range(1, frames):
            total = total + contracted[k, pl.ds(start, rows), :] * normed[k : k + 1, :]
        quarter[...] = total


def second_kernel(scale, where, inverse, *refs):
    pieces, (second, own, packed) = refs[:4], refs[4:]
    gather_rows(where[0], pieces, second, second.shape[0] // QUARTER)
    x = dot(second[...], inverse[...]) * scale
    second[...] = x
    pack_symmetric(dot(x.T, x), packed)
    rows = own.shape[0]
    own[...] = packed[pl.ds(pl.multiple_of(where[0] * rows, rows), rows), :]


def body(tensor, initial_first, initial_second):
    frames, block_first, block_second = tensor.shape
    rank = initial_first.shape[1]
    square, line, column = (rank, rank), (1, rank), (rank, 1)
    packed = (3 * rank // 4, rank)
    half, quarter, eighth = packed[0] // 2, packed[0] // 4, packed[0] // 8
    part = block_second // QUARTER
    rows_first = block_first * lax.axis_size("row")
    rows_second = block_second * lax.axis_size("col")
    at_x = lax.axis_index("row") // 4
    at_core = lax.axis_index("col") % 2
    at_y = lax.axis_index("col") // 2 % QUARTER
    where = jnp.stack([at_x, at_core, at_y]).astype(jnp.int32)

    firsts, seconds = call(
        grams_kernel, "grams", [(eighth, rank), (quarter, rank)], [SMEM] + [VMEM] * 2, [packed]
    )(where, initial_first, initial_second)
    contracted = jnp.einsum("kij,ir->kjr", tensor, initial_first, precision=HIGH)
    terms = jnp.sum(contracted * initial_second[None], axis=1)
    firsts = sum_keeping(jnp.concatenate([firsts, terms], 0), "row", ROW_Z, contracted)
    seconds = jnp.concatenate([seconds, firsts[eighth:]], 0)
    seconds = sum_over(seconds, "col", COL_CORE)
    pieces = jnp.concatenate([seconds, firsts[:eighth]], 0)
    pieces = [pieces] + partners(pieces, "col", COL_Y)
    seconds, firsts = call(
        cross_kernel,
        "cross",
        [seconds.shape, (half, rank)],
        [SMEM] + [VMEM] * 4,
        keep=contracted,
    )(where, *pieces)
    seconds = sum_over(seconds, "col", COL_Z)
    pieces = jnp.concatenate([firsts, seconds], 0)
    pieces = [pieces] + partners(pieces, "row", ROW_X)
    firsts, terms = call(
        split_kernel, "split", [(half, rank), (frames, rank)], [VMEM] * 4, keep=contracted
    )(*pieces)
    (partner,) = partners(firsts, "col", COL_CORE)
    first_gram, state, over_row, over_col = call(
        functools.partial(begin_first_kernel, 1.0 / rows_first, 1.0 / rows_second),
        "begin_first",
        [square, square, line, column],
        [SMEM] + [VMEM] * 6,
        [packed],
    )(where, firsts, partner, *pieces)
    inverse = finish_inverse(state, over_row, over_col, None)
    terms = [terms]
    scaling = jnp.ones(line, F32)

    for repeat in range(PASSES):
        last = repeat == PASSES - 1
        keep = None if last else contracted
        factor_frames, frame_gram, hadamard, own, *sent = call(
            functools.partial(frames_kernel, 1.0 / math.sqrt(rows_first * rows_second)),
            "frames",
            [(frames, rank), square, square] + [(part, rank)] * QUARTER,
            [SMEM] + [VMEM] * (4 + len(terms)),
        )(where, scaling, inverse, first_gram, contracted, *terms)
        sent = [
            lax.ppermute(piece, "row", [(i, i ^ mask) for i in range(lax.axis_size("row"))])
            for piece, mask in zip(sent, ROW_X)
        ]
        state, over_row, over_col = call(
            begin_kernel, "begin", [square, line, column], [VMEM], keep=keep
        )(hadamard)
        own, state = tie(tree([own] + sent), state)
        sums = [own] + partners(own, "row", ROW_Z)
        (state,) = call(middle_kernel, "middle", [square], [VMEM], keep=keep)(state)
        *sums, state = tie(*sums, state)
        piece = tree(sums)
        pieces = [piece] + partners(piece, "row", ROW_X)
        inverse = finish_inverse(state, over_row, over_col, keep)

        second, payload = call(
            functools.partial(second_kernel, 1.0 / math.sqrt(rows_first * frames)),
            "second",
            [(block_second, rank), (quarter, rank)],
            [SMEM] + [VMEM] * 5,
            [packed],
        )(where, inverse, *pieces)
        if not last:
            terms = jnp.sum(contracted * second[None], axis=1)
            payload = jnp.concatenate([payload, terms], 0)
        payload = sum_over(payload, "col", COL_CORE)
        payload = sum_over(payload, "col", COL_Y)
        if last:
            terms = jnp.einsum("kij,jr->kir", tensor, second, precision=HIGH)
            terms = jnp.sum(terms * factor_frames[:, None, :], axis=0)
            terms = sum_over(terms, "col", COL_CORE)
            payload, terms = tie(payload, terms)
            terms = sum_over(terms, "col", COL_Y[:1])
        payload = sum_over(payload, "col", COL_Z)
        sums = [payload] + partners(payload, "row", ROW_X)
        if not last:
            terms = tree([piece[quarter:] for piece in sums])
        *sums, terms = tie(*sums, terms)
        if last:
            terms = sum_over(terms, "col", COL_Y[1:2])
        state, over_row, over_col, scaling = call(
            functools.partial(begin_second_kernel, 1.0 / rows_second),
            "begin_second",
            [square, line, column, line],
            [SMEM] + [VMEM] * 5,
            [packed],
            keep=keep,
        )(where, frame_gram if last else first_gram, *sums)
        if last:
            state, terms = tie(state, terms)
            terms = sum_over(terms, "col", COL_Z)
        else:
            terms = sum_over(terms, "row", ROW_Z[:1])
            state, terms = tie(state, terms)
            terms = [terms] + partners(terms, "row", ROW_Z[1:2])
        inverse = finish_inverse(state, over_row, over_col, keep)

    first_raw = dot(terms / scaling, inverse) * (1.0 / math.sqrt(rows_second * frames))
    squares = jnp.sum(first_raw * first_raw, axis=0, keepdims=True)
    squares = sum_over(sum_over(squares, "row", ROW_X), "row", ROW_Z)
    weights = jnp.sqrt(squares[0] / rows_first + epsilon)
    return (first_raw / weights, second / scaling, factor_frames, weights)


def solution(mesh):
    placed = (P(None, "row", "col"), P("row", None), P("col", None))
    return jax.shard_map(
        body,
        mesh=mesh,
        in_specs=placed,
        out_specs=(P("row", None), P("col", None), P(), P()),
        check_vma=False,
    )
```
